256 devices in a mesh: scen: 16 (over y, x), lx: 4 (over z_lo, core), ly: 4 (over z_hi).
Axes of the slice: x: 4, y: 4, z: 8 (z_hi: 4, z_lo: 2; z = z_hi * 2 + z_lo), core: 2. Of those that a mesh axis runs over, the one named last changes fastest.
Arguments:
- density: float32 [16, 512, 2048], P('scen', 'lx', 'ly'), may hold values from 0.2 to 1.5
- trait: float32 [16, 512, 2048], P('scen', 'lx', 'ly'), may hold values from -4 to 4
- variance: float32 [16, 512, 2048], P('scen', 'lx', 'ly'), may hold values from 0.1 to 1
- optimum: float32 [16, 512, 2048], P('scen', 'lx', 'ly'), may hold values from -4 to 4
- observed: float32 [16, 512, 2048], P('scen', 'lx', 'ly'), may hold values from 0 to 1.5
- obs_step: int32 [16, 512], P('scen', 'lx'), may hold values from 1 to 2
- land_code: int32 [512, 2048], P('lx', 'ly'), may hold values 0 or 1
- maps: float32 [2, 512, 2048], P(None, 'lx', 'ly'), may hold values from -4 to 4
- first_moment: float32 [2, 512, 2048], P(None, 'lx', 'ly'), may hold values from -3 to 3
- second_moment: float32 [2, 512, 2048], P(None, 'lx', 'ly'), may hold values from 0.01 to 1
Outputs:
- new_maps: float32 [2, 512, 2048], P(None, 'lx', 'ly')
- new_first: float32 [2, 512, 2048], P(None, 'lx', 'ly')
- new_second: float32 [2, 512, 2048], P(None, 'lx', 'ly')
The draws below stay inside these ranges and needn't reach their ends.
Inputs may be any that keep to these rules, and one draw needn't show every extreme that they name: `land_code`: 1 marks land, 0 sea.
All inputs are finite; a program needn't handle non-finite values. No bound on the sum of `land_code` on one device may be relied on, other than what follows from the above.
Results may differ from the reference program's by a relative error of at most 0.0003.
Values sent between devices are 32-bit elements; how exact they have to be, the bound alone decides.
A program may use at most 64 MiB of HBM per device.

```python
import math
import jax
import jax.numpy as jnp
from jax import lax

STEPS = 2
ADAM_STEP = 10
SCEN = 16
GX = 512
GY = 2048


def plant(drawn, key, least, top_value):
    shape = drawn.shape
    place = [jax.random.randint(jax.random.fold_in(key, axis), (), 0, shape[axis]) for axis in range(len(shape))]
    drawn = drawn.at[tuple(place)].set(least)
    longest = shape.index(max(shape))
    place[longest] = (place[longest] + 1) % shape[longest]
    return drawn.at[tuple(place)].set(top_value)


def block_levels(rng, extent, cuts, smallest, top_value):
    loudness, own = 1.0, jax.random.fold_in(rng, 6)
    for position, shards_of in cuts:
        heights = jnp.exp(jax.random.uniform(jax.random.fold_in(own, position), (shards_of,), jnp.float32, smallest / len(cuts), top_value / len(cuts)))
        loudness = loudness * jnp.repeat(heights, extent[position] // shards_of).reshape([-1 if axis == position else 1 for axis in range(len(extent))])
    return loudness


def normal_values(stream_key, dims, spread, most, split=(), kind=jnp.bfloat16):
    array = jax.random.normal(stream_key, dims, jnp.float32) * spread
    if len(split) > 0:
        array = block_levels(stream_key, dims, split, -0.22, 0.18) * array
    return jnp.clip(array, min=-most, max=most).astype(kind)


def setup_inputs(seed: int = 0) -> dict:
    key_list = jax.random.split(jax.random.key(seed), 11)
    return {
        "density": jnp.clip(0.2 + 1.3 * jax.random.uniform(key_list[0], (SCEN, GX, GY), jnp.float32) ** block_levels(key_list[0], (SCEN, GX, GY), ((0, 16), (1, 4), (2, 4)), -0.2, 0.2), 0.2, 1.5),
        "trait": normal_values(key_list[1], (SCEN, GX, GY), 1.0, 4.0, ((0, 16), (1, 4), (2, 4)), jnp.float32),
        "variance": jnp.clip(0.1 + 0.9 * jax.random.uniform(key_list[2], (SCEN, GX, GY), jnp.float32) ** block_levels(key_list[2], (SCEN, GX, GY), ((0, 16), (1, 4), (2, 4)), -0.2, 0.2), 0.1, 1.0),
        "optimum": normal_values(key_list[3], (SCEN, GX, GY), 1.0, 4.0, ((0, 16), (1, 4), (2, 4)), jnp.float32),
        "observed": jnp.clip(1.5 * jax.random.uniform(key_list[4], (SCEN, GX, GY), jnp.float32) ** block_levels(key_list[4], (SCEN, GX, GY), ((0, 16), (1, 4), (2, 4)), -0.2, 0.2), 0.0, 1.5),
        "obs_step": plant(jax.random.randint(key_list[5], (SCEN, GX), 1, STEPS + 1), jax.random.fold_in(key_list[5], 1), 1, STEPS).astype(jnp.int32),
        "land_code": plant((jax.random.randint(key_list[6], (GX, GY), 0, 8) < 7).astype(jnp.int32), jax.random.fold_in(key_list[6], 1), 0, 1),
        "maps": normal_values(key_list[7], (2, GX, GY), 1.0, 4.0, ((1, 4), (2, 4)), jnp.float32),
        "first_moment": normal_values(key_list[8], (2, GX, GY), 0.5, 3.0, ((1, 4), (2, 4)), jnp.float32),
        "second_moment": jnp.clip(jnp.exp(math.log(1.0) - 4.6051702 * jax.random.uniform(key_list[9], (2, GX, GY), jnp.float32) ** block_levels(key_list[9], (2, GX, GY), ((1, 4), (2, 4)), -0.2, 0.2)), 0.01, 1.0),
    }


REACH_MAX = 0.2
PRIOR_WEIGHT = 0.1
GROWTH_RATE = 0.5
MUTATION_INPUT = 0.02
LEARN_RATE = 0.01
BETA_FIRST = 0.9
BETA_SECOND = 0.999
ADAM_EPS = 1e-08
LOSS_WEIGHT = 2.0

def interior(values):
    return values[..., 1:-1, 1:-1]

def advance(fields, raw_maps, optimum_map, land_frac):
    density_now, trait_now, variance_now = (fields[0], fields[1], fields[2])
    reach_map = REACH_MAX * jax.nn.sigmoid(raw_maps[0])
    selection = jax.nn.softplus(interior(raw_maps[1]))
    carried = density_now * trait_now
    moment_two = density_now * (variance_now + trait_now * trait_now)
    reach_mid = interior(reach_map)
    land_mid = interior(land_frac)
    cuts = ((slice(2, None), slice(1, -1)), (slice(None, -2), slice(1, -1)), (slice(1, -1), slice(2, None)), (slice(1, -1), slice(None, -2)))
    spread_density = interior(density_now)
    spread_carried = interior(carried)
    spread_moment = interior(moment_two)
    for row_cut, col_cut in cuts:
        weight = 0.5 * (reach_mid + reach_map[row_cut, col_cut]) * land_mid * land_frac[row_cut, col_cut]
        spread_density = spread_density + weight * (density_now[row_cut, col_cut] - interior(density_now))
        spread_carried = spread_carried + weight * (carried[row_cut, col_cut] - interior(carried))
        spread_moment = spread_moment + weight * (moment_two[row_cut, col_cut] - interior(moment_two))
    trait_mid = interior(trait_now)
    variance_mid = interior(variance_now)
    denominator = spread_density + PRIOR_WEIGHT
    trait_spread = (spread_carried + PRIOR_WEIGHT * trait_mid) / denominator
    second_spread = (spread_moment + PRIOR_WEIGHT * (variance_mid + trait_mid * trait_mid)) / denominator
    variance_spread = second_spread - trait_spread * trait_spread
    offset = trait_spread - interior(optimum_map)
    growth = land_mid * (GROWTH_RATE * (1.0 - spread_density) - 0.5 * selection * (offset * offset + variance_spread))
    density_new = spread_density * jnp.exp(growth)
    response = selection * variance_spread
    trait_new = trait_spread - response * offset / (1.0 + response)
    variance_new = variance_spread / (1.0 + response) + MUTATION_INPUT
    return jnp.stack([density_new, trait_new, variance_new])

def adam_update(raw_maps, first_now, second_now, gradient):
    first_new = BETA_FIRST * first_now + (1.0 - BETA_FIRST) * gradient
    second_new = BETA_SECOND * second_now + (1.0 - BETA_SECOND) * gradient * gradient
    first_hat = first_new / (1.0 - BETA_FIRST ** ADAM_STEP)
    second_hat = second_new / (1.0 - BETA_SECOND ** ADAM_STEP)
    maps_new = raw_maps - LEARN_RATE * first_hat / (jnp.sqrt(second_hat) + ADAM_EPS)
    return (maps_new, first_new, second_new)

def pad_cells(values):
    return jnp.pad(values, ((0, 0), (1, 1), (1, 1)))

def scenario_loss(raw_maps, density_s, trait_s, variance_s, optimum_s, observed_s, step_s, land_frac):
    fields = jnp.stack([density_s, trait_s, variance_s])
    loss_total = jnp.float32(0.0)
    for step_index in range(STEPS):
        fields = advance(pad_cells(fields), pad_cells(raw_maps), jnp.pad(optimum_s, 1), jnp.pad(land_frac, 1))
        chosen = (step_s == step_index + 1).astype(jnp.float32)[:, None]
        mismatch = fields[0] - observed_s
        loss_total = loss_total + LOSS_WEIGHT * jnp.sum(chosen * land_frac * mismatch * mismatch)
    return loss_total

def reference(density, trait, variance, optimum, observed, obs_step, land_code, maps, first_moment, second_moment):
    land_frac = land_code.astype(jnp.float32)
    grad_fn = jax.grad(scenario_loss)

    def accumulate(carry_sum, items):
        density_s, trait_s, variance_s, optimum_s, observed_s, step_s = items
        return (carry_sum + grad_fn(maps, density_s, trait_s, variance_s, optimum_s, observed_s, step_s, land_frac), None)
    gradient, _ = lax.scan(accumulate, jnp.zeros(maps.shape, jnp.float32), (density, trait, variance, optimum, observed, obs_step))
    return adam_update(maps, first_moment, second_moment, gradient)
```

```python
import functools

import jax
import jax.numpy as jnp
from jax import lax
from jax.experimental import pallas as pl
from jax.experimental.pallas import tpu as pltpu
from jax.sharding import PartitionSpec as P

ADAM_STEP = 10
REACH_MAX = 0.2
PRIOR = 0.1
GROWTH = 0.5
MUTATION = 0.02
LEARN_RATE = 0.01
BETA_FIRST = 0.9
BETA_SECOND = 0.999
ADAM_EPS = 1e-08
LOSS_WEIGHT = 2.0

MESH = pl.DeviceIdType.MESH
SUB, LANE = 8, 128
BANDS = 4
OFF = 16
DENS, TRAIT, VAR, OPT, OBS, MAP0, MAP1, LAND = range(8)
SIDES = [(-1, -1), (-1, 0), (-1, 1), (0, -1), (0, 1), (1, -1), (1, 0), (1, 1)]
NAMES = (
    "n0", "q0", "m0", "s0", "rho", "lnd", "sel", "wx",
    "wy", "n1", "q1", "m1", "z1", "s1", "e1", "r1",
    "zs1", "ss1", "u1", "fxn", "fxq", "fxm", "gxn", "gxq",
    "gxm", "ln", "lq", "lm", "kn", "kq", "km", "ds",
    "gx", "gy", "hy", "fac0", "fac1",
)
PLANE = {name: index for index, name in enumerate(NAMES)}


def kernel(
    sizes,
    dens,
    trait,
    var,
    opt,
    obs,
    ostep,
    land,
    maps,
    first,
    second,
    o_maps,
    o_first,
    o_second,
    raw,
    rawl,
    own_k,
    up_k,
    down_k,
    krow,
    colsend,
    colrx,
    cornrx,
    square,
    mom,
    planes,
    gsend,
    rrx,
    gfull,
    outs,
    load_sem,
    row_send,
    row_recv,
    col_send,
    col_recv,
    rs_send,
    rs_recv,
    ag_send,
    ag_recv,
    out_sem,
):
    ns, nx, ny, rows, cols = sizes
    tiles = cols // LANE
    wide = tiles + 1
    blocks = rows // SUB
    per_band = blocks // BANDS
    pieces = per_band * tiles // ns
    me_s, me_x, me_y = (lax.axis_index(name) for name in ("scen", "lx", "ly"))
    top, bottom = me_x == 0, me_x == nx - 1
    left, right = me_y == 0, me_y == ny - 1
    lane = lax.broadcasted_iota(jnp.int32, (SUB, LANE), 1)
    sub = lax.broadcasted_iota(jnp.int32, (SUB, LANE), 0)

    def there(dx, dy):
        ok = jnp.bool_(True)
        if dx:
            ok = jnp.logical_not(top if dx < 0 else bottom)
        if dy:
            oky = jnp.logical_not(left if dy < 0 else right)
            ok = jnp.logical_and(ok, oky) if dx else oky
        return ok

    def target(dx, dy):
        return {"lx": me_x + dx, "ly": me_y + dy}

    body = pl.ds(SUB, rows)
    loads = []
    for slot, ref in enumerate((dens, trait, var, opt, obs)):
        loads.append((ref.at[0], raw.at[slot, body, pl.ds(0, cols)]))
    for slot in range(2):
        loads.append((maps.at[slot], raw.at[MAP0 + slot, body, pl.ds(0, cols)]))
    loads.append((land, rawl.at[body, pl.ds(0, cols)]))
    loads.append((ostep, own_k))
    loads.append((first, mom.at[0]))
    loads.append((second, mom.at[1]))
    loads = [
        pltpu.make_async_copy(src, dst, load_sem.at[slot])
        for slot, (src, dst) in enumerate(loads)
    ]
    for copy in loads:
        copy.start()

    barrier = pltpu.get_barrier_semaphore()

    def greet(step, carry):
        pl.semaphore_signal(
            barrier, inc=1, device_id={"scen": lax.rem(me_s + step, ns)}, device_id_type=MESH
        )
        return carry

    lax.fori_loop(1, ns, greet, 0)
    for dx, dy in SIDES:

        @pl.when(there(dx, dy))
        def _(dx=dx, dy=dy):
            pl.semaphore_signal(barrier, inc=1, device_id=target(dx, dy), device_id_type=MESH)

    over_x = jnp.where(top, 0, 1) + jnp.where(bottom, 0, 1)
    over_y = jnp.where(left, 0, 1) + jnp.where(right, 0, 1)
    pl.semaphore_wait(barrier, ns - 1 + (over_x + 1) * (over_y + 1) - 1)

    def row_copies(dx):
        edge = pl.ds(0, SUB) if dx < 0 else pl.ds(rows - SUB, SUB)
        halo = pl.ds(rows + SUB, SUB) if dx < 0 else pl.ds(0, SUB)
        across = pl.ds(0, cols)
        pairs = [
            (ref.at[0, edge, :], raw.at[slot, halo, across])
            for slot, ref in enumerate((dens, trait, var, opt, obs))
        ]
        pairs.append((maps.at[:, edge, :], raw.at[pl.ds(MAP0, 2), halo, across]))
        pairs.append((land.at[edge, :], rawl.at[halo, across]))
        pairs.append((ostep, down_k if dx < 0 else up_k))
        way = 0 if dx < 0 else 1
        return [
            pltpu.make_async_remote_copy(
                src_ref=src,
                dst_ref=dst,
                send_sem=row_send.at[way, slot],
                recv_sem=row_recv.at[way, slot],
                device_id=target(dx, 0),
                device_id_type=MESH,
            )
            for slot, (src, dst) in enumerate(pairs)
        ]

    for dx in (-1, 1):

        @pl.when(there(dx, 0))
        def _(dx=dx):
            for copy in row_copies(dx):
                copy.start()

    for copy in loads[:9]:
        copy.wait()

    def field(slot, rws, cls):
        if slot == LAND:
            return rawl[rws, cls].astype(jnp.float32)
        return raw[slot, rws, cls]

    def pack(block, carry):
        rws = pl.ds(pl.multiple_of(SUB + block * SUB, SUB), SUB)
        packed = jnp.zeros((SUB, LANE), jnp.float32)
        for slot in range(8):
            pair = jnp.where(
                lane < LANE // 2,
                field(slot, rws, pl.ds(0, LANE)),
                field(slot, rws, pl.ds(cols - LANE, LANE)),
            )
            turned = pltpu.roll(pair, 8 * slot + 4, 1)
            packed = jnp.where(lane // 8 == slot, turned, packed)
        square[pl.ds(pl.multiple_of(block * SUB, SUB), SUB), :] = packed
        return carry

    lax.fori_loop(0, blocks, pack, 0)
    turned = jnp.transpose(square[...])
    corner = jnp.zeros((SUB, LANE), jnp.float32)
    for slot in range(8):
        part = turned[8 * slot : 8 * slot + 8, :]
        corner = jnp.where(lane // 8 == slot, pltpu.roll(part, 8 * slot + 4, 1), corner)
    colsend[0:64, :] = turned[0:64, :]
    colsend[64:72, :] = corner

    def col_copy(dx, dy):
        index = SIDES.index((dx, dy))
        came = SIDES.index((-dx, -dy))
        if dx == 0:
            src, dst = colsend.at[0:64, :], colrx.at[0 if dy > 0 else 1]
        else:
            src, dst = colsend.at[64:72, :], cornrx.at[came]
        return pltpu.make_async_remote_copy(
            src_ref=src,
            dst_ref=dst,
            send_sem=col_send.at[index],
            recv_sem=col_recv.at[came],
            device_id=target(dx, dy),
            device_id_type=MESH,
        )

    col_sides = [side for side in SIDES if side[1]]
    for dx, dy in col_sides:

        @pl.when(there(dx, dy))
        def _(dx=dx, dy=dy):
            col_copy(dx, dy).start()

    def prepare(block, lanes):
        src = pl.ds(pl.multiple_of(block * SUB, SUB), SUB)
        dst = pl.ds(pl.multiple_of(block * SUB + OFF - SUB, SUB), SUB)
        for tile in lanes:
            cls = pl.ds(tile * LANE, LANE)
            n, z, v = raw[DENS, src, cls], raw[TRAIT, src, cls], raw[VAR, src, cls]
            second_moment = v + z * z

            def put(name, value):
                planes[PLANE[name], tile, dst, :] = value

            put("n0", n)
            put("q0", n * z)
            put("s0", second_moment)
            put("m0", n * second_moment)
            put("lnd", rawl[src, cls].astype(jnp.float32))
            share = 1.0 / (1.0 + jnp.exp(-raw[MAP0, src, cls]))
            rho = (0.5 * REACH_MAX) * share
            put("rho", rho)
            x = raw[MAP1, src, cls]
            small = jnp.exp(-jnp.abs(x))
            put("sel", jnp.maximum(x, 0.0) + jnp.log1p(small))
            if tile < tiles:
                put("fac0", rho * (1.0 - share))
                put("fac1", jnp.where(x >= 0.0, 1.0, small) / (1.0 + small))

    def prepare_own(block, carry):
        prepare(block, range(tiles))
        return carry

    lax.fori_loop(1, blocks + 1, prepare_own, 0)

    zero = jnp.zeros((SUB, LANE), jnp.float32)
    for dx, halo, kref in ((-1, 0, up_k), (1, rows + SUB, down_k)):

        @pl.when(there(dx, 0))
        def _(dx=dx):
            for copy in row_copies(-dx):
                copy.wait_recv()

        @pl.when(jnp.logical_not(there(dx, 0)))
        def _(halo=halo, kref=kref):
            for tile in range(tiles):
                cls = pl.ds(tile * LANE, LANE)
                for slot in range(7):
                    raw[slot, pl.ds(halo, SUB), cls] = zero
                rawl[pl.ds(halo, SUB), cls] = jnp.zeros((SUB, LANE), jnp.int32)
            kref[...] = jnp.zeros_like(kref)

    for dx, dy in col_sides:

        @pl.when(there(dx, dy))
        def _(dx=dx, dy=dy):
            col_copy(-dx, -dy).wait_recv()

        @pl.when(jnp.logical_not(there(dx, dy)))
        def _(dx=dx, dy=dy):
            if dx == 0:
                colrx[0 if dy < 0 else 1] = jnp.zeros((64, LANE), jnp.float32)
            else:
                cornrx[SIDES.index((dx, dy))] = zero

    for slot in range(8):
        part = pl.ds(8 * slot, 8)
        square[part, :] = jnp.where(sub < 4, colrx[0, part, :], colrx[1, part, :])
    upper = lax.rem(lane, 8) < 4
    square[64:72, :] = jnp.where(
        sub < 4,
        jnp.where(upper, cornrx[SIDES.index((-1, -1))], cornrx[SIDES.index((1, -1))]),
        jnp.where(upper, cornrx[SIDES.index((-1, 1))], cornrx[SIDES.index((1, 1))]),
    )

    def steps_of(ref):
        return jnp.broadcast_to(ref[...], (SUB, LANE)).astype(jnp.float32)

    square[72:80, :] = jnp.where(
        sub == 0,
        steps_of(own_k),
        jnp.where(sub == 1, steps_of(up_k), jnp.where(sub == 2, steps_of(down_k), 0.0)),
    )
    square[80:128, :] = jnp.zeros((48, LANE), jnp.float32)
    square[...] = jnp.transpose(square[...])

    halo_lanes = pl.ds(cols, LANE)

    def put_halo(slot, rws, value):
        if slot == LAND:
            rawl[rws, halo_lanes] = value.astype(jnp.int32)
        else:
            raw[slot, rws, halo_lanes] = value

    def unpack(block, carry):
        got = square[pl.ds(pl.multiple_of(block * SUB, SUB), SUB), :]
        rws = pl.ds(pl.multiple_of(SUB + block * SUB, SUB), SUB)
        for slot in range(8):
            put_halo(slot, rws, pltpu.roll(got, LANE - (8 * slot + 4), 1))
        krow[rws, :] = jnp.broadcast_to(got[:, 72:73], (SUB, LANE))
        return carry

    lax.fori_loop(0, blocks, unpack, 0)
    for slot in range(8):
        got = pltpu.roll(square[8 * slot : 8 * slot + 8, :], LANE - 68, 1)
        got = pltpu.roll(got, 4, 0)
        put_halo(slot, pl.ds(0, SUB), got)
        put_halo(slot, pl.ds(rows + SUB, SUB), got)
    krow[0:SUB, :] = jnp.broadcast_to(square[rows - SUB : rows, 73:74], (SUB, LANE))
    krow[rows + SUB : rows + 2 * SUB, :] = jnp.broadcast_to(square[0:SUB, 74:75], (SUB, LANE))

    def prepare_side(block, carry):
        prepare(block, (tiles,))
        return carry

    lax.fori_loop(0, blocks + 2, prepare_side, 0)
    prepare(0, range(tiles))
    prepare(blocks + 1, range(tiles))

    def east(values):
        turned = [pltpu.roll(value, LANE - 1, 1) for value in values]
        return [
            jnp.where(lane == LANE - 1, turned[(tile + 1) % wide], turned[tile])
            for tile in range(wide)
        ]

    def west(values):
        turned = [pltpu.roll(value, 1, 1) for value in values]
        return [
            jnp.where(lane == 0, turned[(tile - 1) % wide], turned[tile])
            for tile in range(wide)
        ]

    def getter(row):
        def get(name, shift=0):
            if shift == 0:
                rws = pl.ds(pl.multiple_of(row, SUB), SUB)
            else:
                rws = pl.ds(row + shift, SUB)
            return [planes[PLANE[name], tile, rws, :] for tile in range(wide)]

        def put(name, values):
            rws = pl.ds(pl.multiple_of(row, SUB), SUB)
            for tile, value in enumerate(values):
                planes[PLANE[name], tile, rws, :] = value

        def get_raw(slot):
            rws = pl.ds(pl.multiple_of(row - SUB, SUB), SUB)
            return [raw[slot, rws, tile * LANE : (tile + 1) * LANE] for tile in range(wide)]

        return get, put, get_raw

    def spread(get, name, wx, wy, wyn, keep=None, put=None):
        here = get(name)
        fx = [e - c for e, c in zip(east(here), here)]
        if keep is not None:
            put(keep, fx)
        flow = [w * f for w, f in zip(wx, fx)]
        back = west(flow)
        result = [c + (f - b) for c, f, b in zip(here, flow, back)]
        south, north = get(name, 1), get(name, -1)
        result = [
            a + (w * (s - c) + v * (n - c))
            for a, w, s, c, v, n in zip(result, wy, south, here, wyn, north)
        ]
        return result, fx, [s - c for s, c in zip(south, here)]

    def pass_one(block, carry):
        row = block * SUB
        get, put, get_raw = getter(row)
        rho, lnd = get("rho"), get("lnd")
        rho_e, lnd_e = east(rho), east(lnd)
        wx = [(a + b) * (c * d) for a, b, c, d in zip(rho, rho_e, lnd, lnd_e)]
        rho_s, lnd_s = get("rho", 1), get("lnd", 1)
        wy = [(a + b) * (c * d) for a, b, c, d in zip(rho, rho_s, lnd, lnd_s)]
        rho_n, lnd_n = get("rho", -1), get("lnd", -1)
        wyn = [(a + b) * (c * d) for a, b, c, d in zip(rho, rho_n, lnd, lnd_n)]
        put("wx", wx)
        put("wy", wy)
        ns_, _, _ = spread(get, "n0", wx, wy, wyn, "fxn", put)
        qs_, _, _ = spread(get, "q0", wx, wy, wyn, "fxq", put)
        ms_, _, _ = spread(get, "m0", wx, wy, wyn, "fxm", put)
        z, s0, sel, optimum = get_raw(TRAIT), get("s0"), get("sel"), get_raw(OPT)
        rws = pl.ds(pl.multiple_of(row, SUB), SUB)
        for tile in range(wide):

            def one(name, value, tile=tile):
                planes[PLANE[name], tile, rws, :] = value

            recip = 1.0 / (ns_[tile] + PRIOR)
            zs = (qs_[tile] + PRIOR * z[tile]) * recip
            ss = (ms_[tile] + PRIOR * s0[tile]) * recip
            vs = ss - zs * zs
            d = zs - optimum[tile]
            growth = lnd[tile] * (
                GROWTH - GROWTH * ns_[tile] - 0.5 * sel[tile] * (d * d + vs)
            )
            grown = jnp.exp(growth)
            n1 = ns_[tile] * grown
            response = sel[tile] * vs
            u = 1.0 / (1.0 + response)
            z1 = zs - response * u * d
            s1 = vs * u + MUTATION + z1 * z1
            one("e1", grown)
            one("r1", recip)
            one("zs1", zs)
            one("ss1", ss)
            one("u1", u)
            one("n1", n1)
            one("z1", z1)
            one("s1", s1)
            one("q1", n1 * z1)
            one("m1", n1 * s1)
        return carry

    def pass_two(block, carry):
        row = block * SUB
        get, put, get_raw = getter(row)
        wx, wy, wyn = get("wx"), get("wy"), get("wy", -1)
        ns_, _, _ = spread(get, "n1", wx, wy, wyn, "gxn", put)
        qs_, _, _ = spread(get, "q1", wx, wy, wyn, "gxq", put)
        ms_, _, _ = spread(get, "m1", wx, wy, wyn, "gxm", put)
        z, s1, sel, lnd = get("z1"), get("s1"), get("sel"), get("lnd")
        optimum, observed = get_raw(OPT), get_raw(OBS)
        rws = pl.ds(pl.multiple_of(row, SUB), SUB)
        chosen = krow[pl.ds(pl.multiple_of(row - SUB, SUB), SUB), :]
        loss = jnp.where(chosen == 2.0, 2.0 * LOSS_WEIGHT, 0.0)
        for tile in range(wide):

            def one(name, value, tile=tile):
                planes[PLANE[name], tile, rws, :] = value

            recip = 1.0 / (ns_[tile] + PRIOR)
            zs = (qs_[tile] + PRIOR * z[tile]) * recip
            ss = (ms_[tile] + PRIOR * s1[tile]) * recip
            o = optimum[tile]
            phi = ss + o * (o - 2.0 * zs)
            growth = lnd[tile] * (GROWTH - GROWTH * ns_[tile] - 0.5 * sel[tile] * phi)
            grown = jnp.exp(growth)
            n2 = ns_[tile] * grown
            a = (loss * lnd[tile]) * (n2 - observed[tile])
            g = a * n2
            gs = g * sel[tile] * recip
            lq = gs * o
            lm = -0.5 * gs
            one("lq", lq)
            one("lm", lm)
            one("ln", a * grown - 0.5 * g - (zs * lq + ss * lm))
            one("ds", -0.5 * g * phi)
        return carry

    def pass_three(block, carry):
        row = block * SUB
        get, put, get_raw = getter(row)
        wx, wy, wyn = get("wx"), get("wy"), get("wy", -1)
        spreads = []
        gx = gy = None
        for name, state, kept in (("ln", "n1", "gxn"), ("lq", "q1", "gxq"), ("lm", "m1", "gxm")):
            result, fx, fy = spread(get, name, wx, wy, wyn)
            spreads.append(result)
            here, south = get(state), get(state, 1)
            px = [a * b for a, b in zip(fx, get(kept))]
            py = [a * (s - c) for a, s, c in zip(fy, south, here)]
            gx = px if gx is None else [a + b for a, b in zip(gx, px)]
            gy = py if gy is None else [a + b for a, b in zip(gy, py)]
        put("gx", gx)
        put("gy", gy)
        mu_n, mu_q, mu_m = spreads
        names = ("n1", "z1", "s1", "e1", "r1", "zs1", "ss1", "u1", "sel", "lnd", "lq", "lm", "ds")
        vals = {name: get(name) for name in names}
        optimum, observed = get_raw(OPT), get_raw(OBS)
        rws = pl.ds(pl.multiple_of(row, SUB), SUB)
        chosen = krow[pl.ds(pl.multiple_of(row - SUB, SUB), SUB), :]
        loss = jnp.where(chosen == 1.0, 2.0 * LOSS_WEIGHT, 0.0)
        for tile in range(wide):

            def one(name, value, tile=tile):
                planes[PLANE[name], tile, rws, :] = value

            n1, z1, s1, grown, recip, zs, ss, u, sel, lnd, lq, lm, ds = (
                vals[name][tile] for name in names
            )
            c = mu_m[tile] * n1 + PRIOR * lm
            b = mu_q[tile] * n1 + PRIOR * lq + 2.0 * z1 * c
            a = (loss * lnd) * (n1 - observed[tile]) + (
                mu_n[tile] + mu_q[tile] * z1 + mu_m[tile] * s1
            )
            d = zs - optimum[tile]
            vs = ss - zs * zs
            g = a * n1 * lnd
            phi = d * d + vs
            dr = -(u * u) * (b * d + c * vs)
            gs = g * sel
            dd = -(gs * d + b * (1.0 - u))
            dv = c * u + dr * sel - 0.5 * gs
            kq = recip * (b + dd - 2.0 * zs * dv)
            km = recip * dv
            one("kq", kq)
            one("km", km)
            one("kn", a * grown - 0.5 * g - (zs * kq + ss * km))
            one("ds", ds + (dr * vs - 0.5 * g * phi))
        return carry

    def pass_four(block, carry):
        row = block * SUB
        get, put, _ = getter(row)
        gx, gy = get("gx"), get("gy")
        for name, state, kept in (("kn", "n0", "fxn"), ("kq", "q0", "fxq"), ("km", "m0", "fxm")):
            here = get(name)
            fx = get(kept)
            gx = [a + (e - c) * f for a, e, c, f in zip(gx, east(here), here, fx)]
            old = get(state)
            gy = [
                a + (s - c) * (t - o)
                for a, s, c, t, o in zip(gy, get(name, 1), here, get(state, 1), old)
            ]
        lnd, lnd_s = get("lnd"), get("lnd", 1)
        lnd_e = east(lnd)
        hx = [g * (a * b) for g, a, b in zip(gx, lnd, lnd_e)]
        hy = [g * (a * b) for g, a, b in zip(gy, lnd, lnd_s)]
        put("hy", hy)
        total = [a + b + c + d for a, b, c, d in zip(hx, west(hx), hy, get("hy", -1))]
        ds = get("ds")
        rws = pl.ds(pl.multiple_of(row, SUB), SUB)
        for tile in range(tiles):
            gsend[0, tile, rws, :] = -total[tile]
            gsend[1, tile, rws, :] = ds[tile]
        return carry

    def place(owner, piece):
        index = owner * pieces + piece
        return index // tiles, lax.rem(index, tiles)

    def band_rows(band, block, offset):
        return pl.ds(pl.multiple_of(offset + (band * per_band + block) * SUB, SUB), SUB)

    def scatter(band):
        def send(step, carry):
            owner = lax.rem(me_s + step, ns)
            for piece in range(pieces):
                block, tile = place(owner, piece)
                pltpu.make_async_remote_copy(
                    src_ref=gsend.at[:, tile, band_rows(band, block, OFF), :],
                    dst_ref=rrx.at[band, ns - 1 - step, piece],
                    send_sem=rs_send.at[band],
                    recv_sem=rs_recv.at[band],
                    device_id={"scen": owner},
                    device_id_type=MESH,
                ).start()
            return carry

        lax.fori_loop(1, ns, send, 0)

    def all_of(band, sem):
        return pltpu.make_async_copy(rrx.at[band], rrx.at[band], sem.at[band])

    def reduce(band):
        if ns > 1:
            all_of(band, rs_recv).wait()
        for piece in range(pieces):
            block, tile = place(me_s, piece)
            src = band_rows(band, block, OFF)
            for kind in range(2):
                terms = [gsend[kind, tile, src, :]]
                terms += [rrx[band, slot, piece, kind] for slot in range(ns - 1)]
                while len(terms) > 1:
                    pairs = [a + b for a, b in zip(terms[0::2], terms[1::2])]
                    terms = pairs + terms[len(pairs) * 2 :]
                factor = planes[PLANE["fac0"] + kind, tile, src, :]
                gfull[kind, tile, band_rows(band, block, 0), :] = terms[0] * factor

        def send(step, carry):
            other = lax.rem(me_s + step, ns)
            for piece in range(pieces):
                block, tile = place(me_s, piece)
                spot = gfull.at[:, tile, band_rows(band, block, 0), :]
                pltpu.make_async_remote_copy(
                    src_ref=spot,
                    dst_ref=spot,
                    send_sem=ag_send.at[band],
                    recv_sem=ag_recv.at[band],
                    device_id={"scen": other},
                    device_id_type=MESH,
                ).start()
            return carry

        lax.fori_loop(1, ns, send, 0)

    def out_copies(band):
        rws = pl.ds(band * per_band * SUB, per_band * SUB)
        return [
            pltpu.make_async_copy(
                outs.at[index, :, rws, :], ref.at[:, rws, :], out_sem.at[band, index]
            )
            for index, ref in enumerate((o_maps, o_first, o_second))
        ]

    def adam(band):
        if ns > 1:
            all_of(band, ag_recv).wait()

        def update(block, carry):
            rws = pl.ds(pl.multiple_of(block * SUB, SUB), SUB)
            src = pl.ds(pl.multiple_of(block * SUB + SUB, SUB), SUB)
            for kind in range(2):
                for tile in range(tiles):
                    cls = pl.ds(tile * LANE, LANE)
                    g = gfull[kind, tile, rws, :]
                    new_first = BETA_FIRST * mom[0, kind, rws, cls] + (1.0 - BETA_FIRST) * g
                    new_second = (
                        BETA_SECOND * mom[1, kind, rws, cls] + (1.0 - BETA_SECOND) * g * g
                    )
                    root = jnp.sqrt(new_second * (1.0 / (1.0 - BETA_SECOND**ADAM_STEP)))
                    scale = LEARN_RATE / (1.0 - BETA_FIRST**ADAM_STEP)
                    outs[0, kind, rws, cls] = raw[MAP0 + kind, src, cls] - (
                        scale * new_first / (root + ADAM_EPS)
                    )
                    outs[1, kind, rws, cls] = new_first
                    outs[2, kind, rws, cls] = new_second
            return carry

        lax.fori_loop(band * per_band, (band + 1) * per_band, update, 0)
        for copy in out_copies(band):
            copy.start()

    for copy in loads[9:]:
        copy.wait()
    last = blocks + 2
    done = [1, 1, 1, 1]
    for band in range(BANDS):
        top_block = 2 + (band + 1) * per_band
        ends = [min(last + 1, top_block + lead) for lead in (3, 2, 1)] + [top_block]
        for index, step in enumerate((pass_one, pass_two, pass_three, pass_four)):
            lax.fori_loop(done[index], ends[index], step, 0)
        done = ends
        scatter(band)
        if band >= 1:
            reduce(band - 1)
        if band >= 2:
            adam(band - 2)
    reduce(BANDS - 1)
    if BANDS >= 2:
        adam(BANDS - 2)
    adam(BANDS - 1)

    for dx in (-1, 1):

        @pl.when(there(dx, 0))
        def _(dx=dx):
            for copy in row_copies(dx):
                copy.wait_send()

    for dx, dy in col_sides:

        @pl.when(there(dx, dy))
        def _(dx=dx, dy=dy):
            col_copy(dx, dy).wait_send()

    for band in range(BANDS):
        if ns > 1:
            all_of(band, rs_send).wait()
            all_of(band, ag_send).wait()
        for copy in out_copies(band):
            copy.wait()


def solution(mesh):
    ns, nx, ny = (mesh.shape[name] for name in ("scen", "lx", "ly"))

    def shards(density, trait, variance, optimum, observed, obs_step, land_code, maps, first, second):
        _, rows, cols = density.shape
        tiles = cols // LANE
        per_band = rows // SUB // BANDS
        pieces = per_band * tiles // ns
        f32 = jnp.float32
        shape = jax.ShapeDtypeStruct(maps.shape, f32)
        hbm = pl.BlockSpec(memory_space=pl.ANY)
        dma = pltpu.SemaphoreType.DMA
        return pl.pallas_call(
            functools.partial(kernel, (ns, nx, ny, rows, cols)),
            out_shape=(shape, shape, shape),
            in_specs=[hbm] * 10,
            out_specs=(hbm, hbm, hbm),
            scratch_shapes=[
                pltpu.VMEM((7, rows + 2 * SUB, cols + LANE), f32),
                pltpu.VMEM((rows + 2 * SUB, cols + LANE), jnp.int32),
                pltpu.VMEM((1, rows), jnp.int32),
                pltpu.VMEM((1, rows), jnp.int32),
                pltpu.VMEM((1, rows), jnp.int32),
                pltpu.VMEM((rows + 2 * SUB, LANE), f32),
                pltpu.VMEM((72, LANE), f32),
                pltpu.VMEM((2, 64, LANE), f32),
                pltpu.VMEM((8, SUB, LANE), f32),
                pltpu.VMEM((LANE, LANE), f32),
                pltpu.VMEM((2, 2, rows, cols), f32),
                pltpu.VMEM((len(NAMES), tiles + 1, rows + 2 * OFF, LANE), f32),
                pltpu.VMEM((2, tiles, rows + 2 * OFF, LANE), f32),
                pltpu.VMEM((BANDS, max(ns - 1, 1), pieces, 2, SUB, LANE), f32),
                pltpu.VMEM((2, tiles, rows, LANE), f32),
                pltpu.VMEM((3, 2, rows, cols), f32),
                dma((11,)),
                dma((2, 8)),
                dma((2, 8)),
                dma((8,)),
                dma((8,)),
                dma((BANDS,)),
                dma((BANDS,)),
                dma((BANDS,)),
                dma((BANDS,)),
                dma((BANDS, 3)),
            ],
            compiler_params=pltpu.CompilerParams(
                collective_id=0, has_side_effects=True, vmem_limit_bytes=56 * 1024 * 1024
            ),
        )(density, trait, variance, optimum, observed, obs_step, land_code, maps, first, second)

    tile = P("scen", "lx", "ly")
    flat = P(None, "lx", "ly")
    return jax.shard_map(
        shards,
        mesh=mesh,
        in_specs=(tile,) * 5 + (P("scen", "lx"), P("lx", "ly"), flat, flat, flat),
        out_specs=(flat, flat, flat),
        check_vma=False,
    )
```

```python
import functools

import jax
import jax.numpy as jnp
from jax import lax
from jax.experimental import pallas as pl
from jax.experimental.pallas import tpu as pltpu
from jax.sharding import PartitionSpec as P

ADAM_STEP = 10
REACH_MAX = 0.2
PRIOR = 0.1
GROWTH = 0.5
MUTATION = 0.02
LEARN_RATE = 0.01
BETA_FIRST = 0.9
BETA_SECOND = 0.999
ADAM_EPS = 1e-08
LOSS_WEIGHT = 2.0

MESH = pl.DeviceIdType.MESH
SUB, LANE = 8, 128
BANDS = 4
UNROLL = 4
OFF = 16
DENS, TRAIT, VAR, OPT, OBS, MAP0, MAP1, LAND = range(8)
SIDES = [(-1, -1), (-1, 0), (-1, 1), (0, -1), (0, 1), (1, -1), (1, 0), (1, 1)]
NAMES = (
    "n0", "q0", "m0", "s0", "rho", "lnd", "sel", "wx",
    "ww", "wy", "n1", "q1", "m1", "z1", "s1", "e1", "r1",
    "zs1", "ss1", "u1", "fxn", "fxq", "fxm", "gxn", "gxq",
    "gxm", "ln", "lq", "lm", "kn", "kq", "km", "ds",
    "gx", "gy", "hy", "fac0", "fac1",
)
PLANE = {name: index for index, name in enumerate(NAMES)}


def kernel(
    sizes,
    dens,
    trait,
    var,
    opt,
    obs,
    ostep,
    land,
    maps,
    o_grad,
    raw,
    rawl,
    own_k,
    up_k,
    down_k,
    krow,
    colsend,
    cornsend,
    colrx,
    cornrx,
    square,
    gsend,
    rrx,
    total,
    load_sem,
    row_send,
    row_recv,
    col_send,
    col_recv,
    rs_send,
    rs_recv,
    ag_send,
    ag_recv,
    own_sem,
    *planes,
):
    ns, nx, ny, rows, cols = sizes
    tiles = cols // LANE
    wide = tiles + 1
    blocks = rows // SUB
    per_band = blocks // BANDS
    pieces = per_band * tiles // ns
    me_s, me_x, me_y = (lax.axis_index(name) for name in ("scen", "lx", "ly"))
    top, bottom = me_x == 0, me_x == nx - 1
    left, right = me_y == 0, me_y == ny - 1
    lane = lax.broadcasted_iota(jnp.int32, (SUB, LANE), 1)
    sub = lax.broadcasted_iota(jnp.int32, (SUB, LANE), 0)

    def there(dx, dy):
        ok = jnp.bool_(True)
        if dx:
            ok = jnp.logical_not(top if dx < 0 else bottom)
        if dy:
            oky = jnp.logical_not(left if dy < 0 else right)
            ok = jnp.logical_and(ok, oky) if dx else oky
        return ok

    def target(dx, dy):
        return {"lx": me_x + dx, "ly": me_y + dy}

    body = pl.ds(SUB, rows)
    loads = []
    for slot, ref in enumerate((dens, trait, var, opt, obs)):
        loads.append((ref.at[0], raw.at[slot, body, pl.ds(0, cols)]))
    for slot in range(2):
        loads.append((maps.at[slot], raw.at[MAP0 + slot, body, pl.ds(0, cols)]))
    loads.append((land, rawl.at[body, pl.ds(0, cols)]))
    loads.append((ostep, own_k))
    loads = [
        pltpu.make_async_copy(src, dst, load_sem.at[slot])
        for slot, (src, dst) in enumerate(loads)
    ]
    for copy in loads:
        copy.start()

    barrier = pltpu.get_barrier_semaphore()

    def greet(step, carry):
        pl.semaphore_signal(
            barrier, inc=1, device_id={"scen": lax.rem(me_s + step, ns)}, device_id_type=MESH
        )
        return carry

    lax.fori_loop(1, ns, greet, 0)
    for dx, dy in SIDES:

        @pl.when(there(dx, dy))
        def _(dx=dx, dy=dy):
            pl.semaphore_signal(barrier, inc=1, device_id=target(dx, dy), device_id_type=MESH)

    over_x = jnp.where(top, 0, 1) + jnp.where(bottom, 0, 1)
    over_y = jnp.where(left, 0, 1) + jnp.where(right, 0, 1)

    def row_copies(dx):
        edge = pl.ds(0, SUB) if dx < 0 else pl.ds(rows - SUB, SUB)
        halo = pl.ds(rows + SUB, SUB) if dx < 0 else pl.ds(0, SUB)
        across = pl.ds(0, cols)
        pairs = [
            (ref.at[0, edge, :], raw.at[slot, halo, across])
            for slot, ref in enumerate((dens, trait, var, opt, obs))
        ]
        pairs.append((maps.at[:, edge, :], raw.at[pl.ds(MAP0, 2), halo, across]))
        pairs.append((land.at[edge, :], rawl.at[halo, across]))
        pairs.append((ostep, down_k if dx < 0 else up_k))
        way = 0 if dx < 0 else 1
        return [
            pltpu.make_async_remote_copy(
                src_ref=src,
                dst_ref=dst,
                send_sem=row_send.at[way, slot],
                recv_sem=row_recv.at[way, slot],
                device_id=target(dx, 0),
                device_id_type=MESH,
            )
            for slot, (src, dst) in enumerate(pairs)
        ]

    for copy in loads:
        copy.wait()

    def field(slot, rws, cls):
        if slot == LAND:
            return rawl[rws, cls].astype(jnp.float32)
        return raw[slot, rws, cls]

    def pack(block, carry):
        rws = pl.ds(pl.multiple_of(SUB + block * SUB, SUB), SUB)
        packed = jnp.zeros((SUB, LANE), jnp.float32)
        for slot in range(8):
            pair = jnp.where(
                lane < LANE // 2,
                field(slot, rws, pl.ds(0, LANE)),
                field(slot, rws, pl.ds(cols - LANE, LANE)),
            )
            turned = pltpu.roll(pair, 8 * slot + 4, 1)
            packed = jnp.where(lane // 8 == slot, turned, packed)
        square[pl.ds(pl.multiple_of(block * SUB, SUB), SUB), :] = packed
        return carry

    lax.fori_loop(0, blocks, pack, 0)
    turned = jnp.transpose(square[...])
    corner = jnp.zeros((SUB, LANE), jnp.float32)
    for slot in range(8):
        part = turned[8 * slot : 8 * slot + 8, :]
        corner = jnp.where(lane // 8 == slot, pltpu.roll(part, 8 * slot + 4, 1), corner)
    for pair in range(4):
        even = turned[16 * pair : 16 * pair + 8, :]
        odd = turned[16 * pair + 8 : 16 * pair + 16, :]
        colsend[0, 8 * pair : 8 * pair + 8, :] = jnp.where(sub < 4, even, pltpu.roll(odd, 4, 0))
        colsend[1, 8 * pair : 8 * pair + 8, :] = jnp.where(sub < 4, pltpu.roll(even, 4, 0), odd)
    cornsend[...] = corner

    def prepare(block, lanes):
        src = pl.ds(pl.multiple_of(block * SUB, SUB), SUB)
        dst = pl.ds(pl.multiple_of(block * SUB + OFF - SUB, SUB), SUB)
        for tile in lanes:
            cls = pl.ds(tile * LANE, LANE)
            n, z, v = raw[DENS, src, cls], raw[TRAIT, src, cls], raw[VAR, src, cls]
            second_moment = v + z * z

            def put(name, value):
                planes[PLANE[name]][tile, dst, :] = value

            put("n0", n)
            put("q0", n * z)
            put("s0", second_moment)
            put("m0", n * second_moment)
            put("lnd", rawl[src, cls].astype(jnp.float32))
            share = 1.0 / (1.0 + jnp.exp(-raw[MAP0, src, cls]))
            rho = (0.5 * REACH_MAX) * share
            put("rho", rho)
            x = raw[MAP1, src, cls]
            small = jnp.exp(-jnp.abs(x))
            put("sel", jnp.maximum(x, 0.0) + jnp.log1p(small))
            if tile < tiles:
                put("fac0", rho * (1.0 - share))
                put("fac1", jnp.where(x >= 0.0, 1.0, small) / (1.0 + small))

    def prepare_own(block, carry):
        prepare(block, range(tiles))
        return carry


    pl.semaphore_wait(barrier, ns - 1 + (over_x + 1) * (over_y + 1) - 1)
    for dx in (-1, 1):

        @pl.when(there(dx, 0))
        def _(dx=dx):
            for copy in row_copies(dx):
                copy.start()

    def col_copy(dx, dy):
        index = SIDES.index((dx, dy))
        came = SIDES.index((-dx, -dy))
        if dx == 0:
            way = 0 if dy > 0 else 1
            src, dst = colsend.at[way], colrx.at[way]
        else:
            src, dst = cornsend, cornrx.at[came]
        return pltpu.make_async_remote_copy(
            src_ref=src,
            dst_ref=dst,
            send_sem=col_send.at[index],
            recv_sem=col_recv.at[came],
            device_id=target(dx, dy),
            device_id_type=MESH,
        )

    col_sides = [side for side in SIDES if side[1]]
    for dx, dy in col_sides:

        @pl.when(there(dx, dy))
        def _(dx=dx, dy=dy):
            col_copy(dx, dy).start()

    lax.fori_loop(1, blocks + 1, prepare_own, 0)

    zero = jnp.zeros((SUB, LANE), jnp.float32)
    for dx, halo, kref in ((-1, 0, up_k), (1, rows + SUB, down_k)):

        @pl.when(there(dx, 0))
        def _(dx=dx):
            for copy in row_copies(-dx):
                copy.wait_recv()

        @pl.when(jnp.logical_not(there(dx, 0)))
        def _(halo=halo, kref=kref):
            for tile in range(tiles):
                cls = pl.ds(tile * LANE, LANE)
                for slot in range(7):
                    raw[slot, pl.ds(halo, SUB), cls] = zero
                rawl[pl.ds(halo, SUB), cls] = jnp.zeros((SUB, LANE), jnp.int32)
            kref[...] = jnp.zeros_like(kref)

    for dx, dy in col_sides:

        @pl.when(there(dx, dy))
        def _(dx=dx, dy=dy):
            col_copy(-dx, -dy).wait_recv()

        @pl.when(jnp.logical_not(there(dx, dy)))
        def _(dx=dx, dy=dy):
            if dx == 0:
                colrx[0 if dy < 0 else 1] = jnp.zeros((32, LANE), jnp.float32)
            else:
                cornrx[SIDES.index((dx, dy))] = zero

    for pair in range(4):
        part = pl.ds(8 * pair, 8)
        from_left, from_right = colrx[0, part, :], colrx[1, part, :]
        square[16 * pair : 16 * pair + 8, :] = jnp.where(
            sub < 4, from_left, pltpu.roll(from_right, 4, 0)
        )
        square[16 * pair + 8 : 16 * pair + 16, :] = jnp.where(
            sub < 4, pltpu.roll(from_left, 4, 0), from_right
        )
    upper = lax.rem(lane, 8) < 4
    square[64:72, :] = jnp.where(
        sub < 4,
        jnp.where(upper, cornrx[SIDES.index((-1, -1))], cornrx[SIDES.index((1, -1))]),
        jnp.where(upper, cornrx[SIDES.index((-1, 1))], cornrx[SIDES.index((1, 1))]),
    )

    def steps_of(ref):
        return jnp.broadcast_to(ref[...], (SUB, LANE)).astype(jnp.float32)

    square[72:80, :] = jnp.where(
        sub == 0,
        steps_of(own_k),
        jnp.where(sub == 1, steps_of(up_k), jnp.where(sub == 2, steps_of(down_k), 0.0)),
    )
    square[80:128, :] = jnp.zeros((48, LANE), jnp.float32)
    square[...] = jnp.transpose(square[...])

    halo_lanes = pl.ds(cols, LANE)

    def put_halo(slot, rws, value):
        if slot == LAND:
            rawl[rws, halo_lanes] = value.astype(jnp.int32)
        else:
            raw[slot, rws, halo_lanes] = value

    def unpack(block, carry):
        got = square[pl.ds(pl.multiple_of(block * SUB, SUB), SUB), :]
        rws = pl.ds(pl.multiple_of(SUB + block * SUB, SUB), SUB)
        for slot in range(8):
            put_halo(slot, rws, pltpu.roll(got, LANE - (8 * slot + 4), 1))
        krow[rws, :] = jnp.broadcast_to(got[:, 72:73], (SUB, LANE))
        return carry

    lax.fori_loop(0, blocks, unpack, 0)
    for slot in range(8):
        got = pltpu.roll(square[8 * slot : 8 * slot + 8, :], LANE - 68, 1)
        got = pltpu.roll(got, 4, 0)
        put_halo(slot, pl.ds(0, SUB), got)
        put_halo(slot, pl.ds(rows + SUB, SUB), got)
    krow[0:SUB, :] = jnp.broadcast_to(square[rows - SUB : rows, 73:74], (SUB, LANE))
    krow[rows + SUB : rows + 2 * SUB, :] = jnp.broadcast_to(square[0:SUB, 74:75], (SUB, LANE))

    def prepare_side(block, carry):
        prepare(block, (tiles,))
        return carry

    lax.fori_loop(0, blocks + 2, prepare_side, 0)
    prepare(0, range(tiles))
    prepare(blocks + 1, range(tiles))

    def east(values):
        turned = [pltpu.roll(value, LANE - 1, 1) for value in values]
        return [
            jnp.where(lane == LANE - 1, turned[(tile + 1) % wide], turned[tile])
            for tile in range(wide)
        ]

    def west(values):
        turned = [pltpu.roll(value, 1, 1) for value in values]
        return [
            jnp.where(lane == 0, turned[(tile - 1) % wide], turned[tile])
            for tile in range(wide)
        ]

    def getter(row):
        def get(name, shift=0):
            if shift == 0:
                rws = pl.ds(pl.multiple_of(row, SUB), SUB)
            else:
                rws = pl.ds(row + shift, SUB)
            return [planes[PLANE[name]][tile, rws, :] for tile in range(wide)]

        def put(name, values):
            rws = pl.ds(pl.multiple_of(row, SUB), SUB)
            for tile, value in enumerate(values):
                planes[PLANE[name]][tile, rws, :] = value

        def get_raw(slot):
            rws = pl.ds(pl.multiple_of(row - SUB, SUB), SUB)
            return [raw[slot, rws, tile * LANE : (tile + 1) * LANE] for tile in range(wide)]

        return get, put, get_raw

    def spread(get, name, weights, keep=None, put=None):
        wx, ww, wy, wyn = weights
        here = get(name)
        ahead, behind = east(here), west(here)
        south, north = get(name, 1), get(name, -1)
        fx = [e - c for e, c in zip(ahead, here)]
        fy = [s - c for s, c in zip(south, here)]
        if keep is not None:
            put(keep, fx)
        result = [
            c + ((w * f + v * (b - c)) + (y * g + u * (n - c)))
            for c, w, f, v, b, y, g, u, n in zip(here, wx, fx, ww, behind, wy, fy, wyn, north)
        ]
        return result, fx, fy

    def pass_one(block, carry):
        row = block * SUB
        get, put, get_raw = getter(row)
        rho, lnd = get("rho"), get("lnd")
        rho_e, lnd_e = east(rho), east(lnd)
        wx = [(a + b) * (c * d) for a, b, c, d in zip(rho, rho_e, lnd, lnd_e)]
        rho_s, lnd_s = get("rho", 1), get("lnd", 1)
        wy = [(a + b) * (c * d) for a, b, c, d in zip(rho, rho_s, lnd, lnd_s)]
        rho_n, lnd_n = get("rho", -1), get("lnd", -1)
        wyn = [(a + b) * (c * d) for a, b, c, d in zip(rho, rho_n, lnd, lnd_n)]
        ww = west(wx)
        put("wx", wx)
        put("ww", ww)
        put("wy", wy)
        weights = (wx, ww, wy, wyn)
        ns_, _, _ = spread(get, "n0", weights, "fxn", put)
        qs_, _, _ = spread(get, "q0", weights, "fxq", put)
        ms_, _, _ = spread(get, "m0", weights, "fxm", put)
        z, s0, sel, optimum = get_raw(TRAIT), get("s0"), get("sel"), get_raw(OPT)
        rws = pl.ds(pl.multiple_of(row, SUB), SUB)
        for tile in range(wide):

            def one(name, value, tile=tile):
                planes[PLANE[name]][tile, rws, :] = value

            recip = 1.0 / (ns_[tile] + PRIOR)
            zs = (qs_[tile] + PRIOR * z[tile]) * recip
            ss = (ms_[tile] + PRIOR * s0[tile]) * recip
            vs = ss - zs * zs
            d = zs - optimum[tile]
            growth = lnd[tile] * (
                GROWTH - GROWTH * ns_[tile] - 0.5 * sel[tile] * (d * d + vs)
            )
            grown = jnp.exp(growth)
            n1 = ns_[tile] * grown
            response = sel[tile] * vs
            u = 1.0 / (1.0 + response)
            z1 = zs - response * u * d
            s1 = vs * u + MUTATION + z1 * z1
            one("e1", grown)
            one("r1", recip)
            one("zs1", zs)
            one("ss1", ss)
            one("u1", u)
            one("n1", n1)
            one("z1", z1)
            one("s1", s1)
            one("q1", n1 * z1)
            one("m1", n1 * s1)
        return carry

    def pass_two(block, carry):
        row = block * SUB
        get, put, get_raw = getter(row)
        weights = (get("wx"), get("ww"), get("wy"), get("wy", -1))
        ns_, _, _ = spread(get, "n1", weights, "gxn", put)
        qs_, _, _ = spread(get, "q1", weights, "gxq", put)
        ms_, _, _ = spread(get, "m1", weights, "gxm", put)
        z, s1, sel, lnd = get("z1"), get("s1"), get("sel"), get("lnd")
        optimum, observed = get_raw(OPT), get_raw(OBS)
        rws = pl.ds(pl.multiple_of(row, SUB), SUB)
        chosen = krow[pl.ds(pl.multiple_of(row - SUB, SUB), SUB), :]
        loss = jnp.where(chosen == 2.0, 2.0 * LOSS_WEIGHT, 0.0)
        for tile in range(wide):

            def one(name, value, tile=tile):
                planes[PLANE[name]][tile, rws, :] = value

            recip = 1.0 / (ns_[tile] + PRIOR)
            zs = (qs_[tile] + PRIOR * z[tile]) * recip
            ss = (ms_[tile] + PRIOR * s1[tile]) * recip
            o = optimum[tile]
            phi = ss + o * (o - 2.0 * zs)
            growth = lnd[tile] * (GROWTH - GROWTH * ns_[tile] - 0.5 * sel[tile] * phi)
            grown = jnp.exp(growth)
            n2 = ns_[tile] * grown
            a = (loss * lnd[tile]) * (n2 - observed[tile])
            g = a * n2
            gs = g * sel[tile] * recip
            lq = gs * o
            lm = -0.5 * gs
            one("lq", lq)
            one("lm", lm)
            one("ln", a * grown - 0.5 * g - (zs * lq + ss * lm))
            one("ds", -0.5 * g * phi)
        return carry

    def pass_three(block, carry):
        row = block * SUB
        get, put, get_raw = getter(row)
        weights = (get("wx"), get("ww"), get("wy"), get("wy", -1))
        spreads = []
        gx = gy = None
        for name, state, kept in (("ln", "n1", "gxn"), ("lq", "q1", "gxq"), ("lm", "m1", "gxm")):
            result, fx, fy = spread(get, name, weights)
            spreads.append(result)
            here, south = get(state), get(state, 1)
            px = [a * b for a, b in zip(fx, get(kept))]
            py = [a * (s - c) for a, s, c in zip(fy, south, here)]
            gx = px if gx is None else [a + b for a, b in zip(gx, px)]
            gy = py if gy is None else [a + b for a, b in zip(gy, py)]
        put("gx", gx)
        put("gy", gy)
        mu_n, mu_q, mu_m = spreads
        names = ("n1", "z1", "s1", "e1", "r1", "zs1", "ss1", "u1", "sel", "lnd", "lq", "lm", "ds")
        vals = {name: get(name) for name in names}
        optimum, observed = get_raw(OPT), get_raw(OBS)
        rws = pl.ds(pl.multiple_of(row, SUB), SUB)
        chosen = krow[pl.ds(pl.multiple_of(row - SUB, SUB), SUB), :]
        loss = jnp.where(chosen == 1.0, 2.0 * LOSS_WEIGHT, 0.0)
        for tile in range(wide):

            def one(name, value, tile=tile):
                planes[PLANE[name]][tile, rws, :] = value

            n1, z1, s1, grown, recip, zs, ss, u, sel, lnd, lq, lm, ds = (
                vals[name][tile] for name in names
            )
            c = mu_m[tile] * n1 + PRIOR * lm
            b = mu_q[tile] * n1 + PRIOR * lq + 2.0 * z1 * c
            a = (loss * lnd) * (n1 - observed[tile]) + (
                mu_n[tile] + mu_q[tile] * z1 + mu_m[tile] * s1
            )
            d = zs - optimum[tile]
            vs = ss - zs * zs
            g = a * n1 * lnd
            phi = d * d + vs
            dr = -(u * u) * (b * d + c * vs)
            gs = g * sel
            dd = -(gs * d + b * (1.0 - u))
            dv = c * u + dr * sel - 0.5 * gs
            kq = recip * (b + dd - 2.0 * zs * dv)
            km = recip * dv
            one("kq", kq)
            one("km", km)
            one("kn", a * grown - 0.5 * g - (zs * kq + ss * km))
            one("ds", ds + (dr * vs - 0.5 * g * phi))
        return carry

    def pass_four(block, carry):
        row = block * SUB
        get, put, _ = getter(row)
        gx, gy = get("gx"), get("gy")
        for name, state, kept in (("kn", "n0", "fxn"), ("kq", "q0", "fxq"), ("km", "m0", "fxm")):
            here = get(name)
            fx = get(kept)
            gx = [a + (e - c) * f for a, e, c, f in zip(gx, east(here), here, fx)]
            old = get(state)
            gy = [
                a + (s - c) * (t - o)
                for a, s, c, t, o in zip(gy, get(name, 1), here, get(state, 1), old)
            ]
        lnd, lnd_s = get("lnd"), get("lnd", 1)
        lnd_e = east(lnd)
        hx = [g * (a * b) for g, a, b in zip(gx, lnd, lnd_e)]
        hy = [g * (a * b) for g, a, b in zip(gy, lnd, lnd_s)]
        put("hy", hy)
        total = [a + b + c + d for a, b, c, d in zip(hx, west(hx), hy, get("hy", -1))]
        ds = get("ds")
        rws = pl.ds(pl.multiple_of(row, SUB), SUB)
        for tile in range(tiles):
            gsend[0, tile, rws, :] = -total[tile]
            gsend[1, tile, rws, :] = ds[tile]
        return carry

    def place(owner, piece):
        index = owner * pieces + piece
        return index // tiles, lax.rem(index, tiles)

    def band_rows(band, block, offset):
        return pl.ds(pl.multiple_of(offset + (band * per_band + block) * SUB, SUB), SUB)

    def scatter(band):
        def send(step, carry):
            owner = lax.rem(me_s + step, ns)
            for piece in range(pieces):
                block, tile = place(owner, piece)
                pltpu.make_async_remote_copy(
                    src_ref=gsend.at[:, tile, band_rows(band, block, OFF), :],
                    dst_ref=rrx.at[band, ns - 1 - step, piece],
                    send_sem=rs_send.at[band],
                    recv_sem=rs_recv.at[band],
                    device_id={"scen": owner},
                    device_id_type=MESH,
                ).start()
            return carry

        lax.fori_loop(1, ns, send, 0)

    def all_of(band, sem):
        return pltpu.make_async_copy(rrx.at[band], rrx.at[band], sem.at[band])

    def reduce(band):
        if ns > 1:
            all_of(band, rs_recv).wait()
        for piece in range(pieces):
            block, tile = place(me_s, piece)
            src = band_rows(band, block, OFF)
            for kind in range(2):
                terms = [gsend[kind, tile, src, :]]
                terms += [rrx[band, slot, piece, kind] for slot in range(ns - 1)]
                while len(terms) > 1:
                    pairs = [a + b for a, b in zip(terms[0::2], terms[1::2])]
                    terms = pairs + terms[len(pairs) * 2 :]
                factor = planes[PLANE["fac0"] + kind][tile, src, :]
                total[band, piece, kind] = terms[0] * factor

        def send(step, carry):
            other = lax.rem(me_s + step, ns)
            for piece in range(pieces):
                pltpu.make_async_remote_copy(
                    src_ref=total.at[band, piece],
                    dst_ref=spot(band, piece),
                    send_sem=ag_send.at[band],
                    recv_sem=ag_recv.at[band],
                    device_id={"scen": other},
                    device_id_type=MESH,
                ).start()
            return carry

        lax.fori_loop(1, ns, send, 0)
        for piece in range(pieces):
            own_copy(band, piece).start()

    def spot(band, piece):
        block, tile = place(me_s, piece)
        across = pl.ds(pl.multiple_of(tile * LANE, LANE), LANE)
        return o_grad.at[:, band_rows(band, block, 0), across]

    def own_copy(band, piece):
        return pltpu.make_async_copy(
            total.at[band, piece], spot(band, piece), own_sem.at[band, piece]
        )

    def run(step, start, stop):
        whole = (stop - start) // UNROLL

        def several(count):
            def body(index, carry):
                for part in range(count):
                    step(start + index * UNROLL + part, 0)
                return carry

            return body

        if whole > 0:
            lax.fori_loop(0, whole, several(UNROLL), 0)
        rest = (stop - start) - whole * UNROLL
        if rest > 0:
            several(rest)(jnp.int32(whole), 0)

    last = blocks + 2
    done = [1, 1, 1, 1]
    for band in range(BANDS):
        top_block = 2 + (band + 1) * per_band
        ends = [min(last + 1, top_block + lead) for lead in (3, 2, 1)] + [top_block]
        for index, step in enumerate((pass_one, pass_two, pass_three, pass_four)):
            run(step, done[index], ends[index])
        done = ends
        scatter(band)
        if band >= 1:
            reduce(band - 1)
    reduce(BANDS - 1)

    for dx in (-1, 1):

        @pl.when(there(dx, 0))
        def _(dx=dx):
            for copy in row_copies(dx):
                copy.wait_send()

    for dx, dy in col_sides:

        @pl.when(there(dx, dy))
        def _(dx=dx, dy=dy):
            col_copy(dx, dy).wait_send()

    for band in range(BANDS):
        if ns > 1:
            all_of(band, rs_send).wait()
            all_of(band, ag_send).wait()
            all_of(band, ag_recv).wait()
        for piece in range(pieces):
            own_copy(band, piece).wait()


def solution(mesh):
    ns, nx, ny = (mesh.shape[name] for name in ("scen", "lx", "ly"))

    def shards(density, trait, variance, optimum, observed, obs_step, land_code, maps, first, second):
        _, rows, cols = density.shape
        tiles = cols // LANE
        per_band = rows // SUB // BANDS
        pieces = per_band * tiles // ns
        f32 = jnp.float32
        shape = jax.ShapeDtypeStruct(maps.shape, f32)
        dma = pltpu.SemaphoreType.DMA
        gradient = pl.pallas_call(
            functools.partial(kernel, (ns, nx, ny, rows, cols)),
            out_shape=shape,
            in_specs=[pl.BlockSpec(memory_space=pltpu.HBM)] * 8,
            out_specs=pl.BlockSpec(memory_space=pl.ANY),
            scratch_shapes=[
                pltpu.VMEM((7, rows + 2 * SUB, cols + LANE), f32),
                pltpu.VMEM((rows + 2 * SUB, cols + LANE), jnp.int32),
                pltpu.VMEM((1, rows), jnp.int32),
                pltpu.VMEM((1, rows), jnp.int32),
                pltpu.VMEM((1, rows), jnp.int32),
                pltpu.VMEM((rows + 2 * SUB, LANE), f32),
                pltpu.VMEM((2, 32, LANE), f32),
                pltpu.VMEM((SUB, LANE), f32),
                pltpu.VMEM((2, 32, LANE), f32),
                pltpu.VMEM((8, SUB, LANE), f32),
                pltpu.VMEM((LANE, LANE), f32),
                pltpu.VMEM((2, tiles, rows + 2 * OFF, LANE), f32),
                pltpu.VMEM((BANDS, max(ns - 1, 1), pieces, 2, SUB, LANE), f32),
                pltpu.VMEM((BANDS, pieces, 2, SUB, LANE), f32),
                dma((9,)),
                dma((2, 8)),
                dma((2, 8)),
                dma((8,)),
                dma((8,)),
                dma((BANDS,)),
                dma((BANDS,)),
                dma((BANDS,)),
                dma((BANDS,)),
                dma((BANDS, pieces)),
            ]
            + [pltpu.VMEM((tiles + 1, rows + 2 * OFF, LANE), f32)] * len(NAMES),
            compiler_params=pltpu.CompilerParams(
                collective_id=0, has_side_effects=True, vmem_limit_bytes=60 * 1024 * 1024
            ),
        )(density, trait, variance, optimum, observed, obs_step, land_code, maps)
        new_first = BETA_FIRST * first + (1.0 - BETA_FIRST) * gradient
        new_second = BETA_SECOND * second + (1.0 - BETA_SECOND) * gradient * gradient
        first_hat = new_first / (1.0 - BETA_FIRST**ADAM_STEP)
        second_hat = new_second / (1.0 - BETA_SECOND**ADAM_STEP)
        new_maps = maps - LEARN_RATE * first_hat / (jnp.sqrt(second_hat) + ADAM_EPS)
        return new_maps, new_first, new_second

    tile = P("scen", "lx", "ly")
    flat = P(None, "lx", "ly")
    return jax.shard_map(
        shards,
        mesh=mesh,
        in_specs=(tile,) * 5 + (P("scen", "lx"), P("lx", "ly"), flat, flat, flat),
        out_specs=(flat, flat, flat),
        check_vma=False,
    )
```

```python
import functools

import jax
import jax.numpy as jnp
from jax import lax
from jax.experimental import pallas as pl
from jax.experimental.pallas import tpu as pltpu
from jax.sharding import PartitionSpec as P

ADAM_STEP = 10
REACH_MAX = 0.2
PRIOR = 0.1
GROWTH = 0.5
MUTATION = 0.02
LEARN_RATE = 0.01
BETA_FIRST = 0.9
BETA_SECOND = 0.999
ADAM_EPS = 1e-08
LOSS_WEIGHT = 2.0

MESH = pl.DeviceIdType.MESH
SUB, LANE = 8, 128
HALO = 4
BANDS = 4
UNROLL = 4
OFF = 16
DENS, TRAIT, VAR, OPT, OBS, MAP0, MAP1, LAND = range(8)
SIDES = [(-1, -1), (-1, 0), (-1, 1), (0, -1), (0, 1), (1, -1), (1, 0), (1, 1)]
NAMES = (
    "n0", "q0", "m0", "s0", "rho", "lnd", "sel", "wx",
    "ww", "wy", "n1", "q1", "m1", "z1", "s1", "e1", "r1",
    "zs1", "ss1", "u1", "fxn", "fxq", "fxm", "gxn", "gxq",
    "gxm", "ln", "lq", "lm", "kn", "kq", "km", "ds",
    "gx", "gy", "hy", "fac0", "fac1",
)
PLANE = {name: index for index, name in enumerate(NAMES)}


def kernel(
    sizes,
    dens,
    trait,
    var,
    opt,
    obs,
    ostep,
    land,
    maps,
    o_grad,
    raw,
    rawl,
    own_k,
    up_k,
    down_k,
    krow,
    colsend,
    cornsend,
    colrx,
    cornrx,
    square,
    gsend,
    rrx,
    total,
    load_sem,
    row_send,
    row_recv,
    col_send,
    col_recv,
    rs_send,
    rs_recv,
    ag_send,
    ag_recv,
    own_sem,
    *planes,
):
    ns, nx, ny, rows, cols = sizes
    tiles = cols // LANE
    wide = tiles + 1
    blocks = rows // SUB
    per_band = blocks // BANDS
    pieces = per_band * tiles // ns
    me_s, me_x, me_y = (lax.axis_index(name) for name in ("scen", "lx", "ly"))
    top, bottom = me_x == 0, me_x == nx - 1
    left, right = me_y == 0, me_y == ny - 1
    lane = lax.broadcasted_iota(jnp.int32, (SUB, LANE), 1)
    sub = lax.broadcasted_iota(jnp.int32, (SUB, LANE), 0)

    def there(dx, dy):
        ok = jnp.bool_(True)
        if dx:
            ok = jnp.logical_not(top if dx < 0 else bottom)
        if dy:
            oky = jnp.logical_not(left if dy < 0 else right)
            ok = jnp.logical_and(ok, oky) if dx else oky
        return ok

    def target(dx, dy):
        return {"lx": me_x + dx, "ly": me_y + dy}

    body = pl.ds(SUB, rows)
    loads = []
    for slot, ref in enumerate((dens, trait, var, opt, obs)):
        loads.append((ref.at[0], raw.at[slot, body, pl.ds(0, cols)]))
    for slot in range(2):
        loads.append((maps.at[slot], raw.at[MAP0 + slot, body, pl.ds(0, cols)]))
    loads.append((land, rawl.at[body, pl.ds(0, cols)]))
    loads.append((ostep, own_k))
    loads = [
        pltpu.make_async_copy(src, dst, load_sem.at[slot])
        for slot, (src, dst) in enumerate(loads)
    ]
    for copy in loads:
        copy.start()

    barrier = pltpu.get_barrier_semaphore()

    def greet(step, carry):
        pl.semaphore_signal(
            barrier, inc=1, device_id={"scen": lax.rem(me_s + step, ns)}, device_id_type=MESH
        )
        return carry

    lax.fori_loop(1, ns, greet, 0)
    for dx, dy in SIDES:

        @pl.when(there(dx, dy))
        def _(dx=dx, dy=dy):
            pl.semaphore_signal(barrier, inc=1, device_id=target(dx, dy), device_id_type=MESH)

    over_x = jnp.where(top, 0, 1) + jnp.where(bottom, 0, 1)
    over_y = jnp.where(left, 0, 1) + jnp.where(right, 0, 1)

    def row_copies(dx):
        edge = pl.ds(0, HALO) if dx < 0 else pl.ds(rows - HALO, HALO)
        halo = pl.ds(rows + SUB, HALO) if dx < 0 else pl.ds(SUB - HALO, HALO)
        across = pl.ds(0, cols)
        pairs = [
            (ref.at[0, edge, :], raw.at[slot, halo, across])
            for slot, ref in enumerate((dens, trait, var, opt, obs))
        ]
        pairs.append((maps.at[:, edge, :], raw.at[pl.ds(MAP0, 2), halo, across]))
        pairs.append((land.at[edge, :], rawl.at[halo, across]))
        pairs.append((ostep, down_k if dx < 0 else up_k))
        way = 0 if dx < 0 else 1
        return [
            pltpu.make_async_remote_copy(
                src_ref=src,
                dst_ref=dst,
                send_sem=row_send.at[way, slot],
                recv_sem=row_recv.at[way, slot],
                device_id=target(dx, 0),
                device_id_type=MESH,
            )
            for slot, (src, dst) in enumerate(pairs)
        ]

    for copy in loads:
        copy.wait()

    def field(slot, rws, cls):
        if slot == LAND:
            return rawl[rws, cls].astype(jnp.float32)
        return raw[slot, rws, cls]

    def pack(block, carry):
        rws = pl.ds(pl.multiple_of(SUB + block * SUB, SUB), SUB)
        packed = jnp.zeros((SUB, LANE), jnp.float32)
        for slot in range(8):
            pair = jnp.where(
                lane < LANE // 2,
                field(slot, rws, pl.ds(0, LANE)),
                field(slot, rws, pl.ds(cols - LANE, LANE)),
            )
            turned = pltpu.roll(pair, 8 * slot + 4, 1)
            packed = jnp.where(lane // 8 == slot, turned, packed)
        square[pl.ds(pl.multiple_of(block * SUB, SUB), SUB), :] = packed
        return carry

    lax.fori_loop(0, blocks, pack, 0, unroll=4)
    turned = jnp.transpose(square[...])
    corner = jnp.zeros((SUB, LANE), jnp.float32)
    for slot in range(8):
        part = turned[8 * slot : 8 * slot + 8, :]
        corner = jnp.where(lane // 8 == slot, pltpu.roll(part, 8 * slot + 4, 1), corner)
    for pair in range(4):
        even = turned[16 * pair : 16 * pair + 8, :]
        odd = turned[16 * pair + 8 : 16 * pair + 16, :]
        colsend[0, 8 * pair : 8 * pair + 8, :] = jnp.where(sub < 4, even, pltpu.roll(odd, 4, 0))
        colsend[1, 8 * pair : 8 * pair + 8, :] = jnp.where(sub < 4, pltpu.roll(even, 4, 0), odd)
    cornsend[...] = corner

    def prepare(block, lanes):
        src = pl.ds(pl.multiple_of(block * SUB, SUB), SUB)
        dst = pl.ds(pl.multiple_of(block * SUB + OFF - SUB, SUB), SUB)
        for tile in lanes:
            cls = pl.ds(tile * LANE, LANE)
            n, z, v = raw[DENS, src, cls], raw[TRAIT, src, cls], raw[VAR, src, cls]
            second_moment = v + z * z

            def put(name, value):
                planes[PLANE[name]][tile, dst, :] = value

            put("n0", n)
            put("q0", n * z)
            put("s0", second_moment)
            put("m0", n * second_moment)
            put("lnd", rawl[src, cls].astype(jnp.float32))
            share = 1.0 / (1.0 + jnp.exp(-raw[MAP0, src, cls]))
            rho = (0.5 * REACH_MAX) * share
            put("rho", rho)
            x = raw[MAP1, src, cls]
            small = jnp.exp(-jnp.abs(x))
            put("sel", jnp.maximum(x, 0.0) + jnp.log1p(small))
            if tile < tiles:
                put("fac0", rho * (1.0 - share))
                put("fac1", jnp.where(x >= 0.0, 1.0, small) / (1.0 + small))

    def prepare_own(block, carry):
        prepare(block, range(tiles))
        return carry


    pl.semaphore_wait(barrier, ns - 1 + (over_x + 1) * (over_y + 1) - 1)
    for dx in (-1, 1):

        @pl.when(there(dx, 0))
        def _(dx=dx):
            for copy in row_copies(dx):
                copy.start()

    def col_copy(dx, dy):
        index = SIDES.index((dx, dy))
        came = SIDES.index((-dx, -dy))
        if dx == 0:
            way = 0 if dy > 0 else 1
            src, dst = colsend.at[way], colrx.at[way]
        else:
            src, dst = cornsend, cornrx.at[came]
        return pltpu.make_async_remote_copy(
            src_ref=src,
            dst_ref=dst,
            send_sem=col_send.at[index],
            recv_sem=col_recv.at[came],
            device_id=target(dx, dy),
            device_id_type=MESH,
        )

    col_sides = [side for side in SIDES if side[1]]
    for dx, dy in col_sides:

        @pl.when(there(dx, dy))
        def _(dx=dx, dy=dy):
            col_copy(dx, dy).start()

    lax.fori_loop(1, blocks + 1, prepare_own, 0, unroll=4)

    zero = jnp.zeros((SUB, LANE), jnp.float32)
    for dx, halo, kref in ((-1, 0, up_k), (1, rows + SUB, down_k)):

        @pl.when(there(dx, 0))
        def _(dx=dx):
            for copy in row_copies(-dx):
                copy.wait_recv()

        @pl.when(jnp.logical_not(there(dx, 0)))
        def _(halo=halo, kref=kref):
            for tile in range(tiles):
                cls = pl.ds(tile * LANE, LANE)
                for slot in range(7):
                    raw[slot, pl.ds(halo, SUB), cls] = zero
                rawl[pl.ds(halo, SUB), cls] = jnp.zeros((SUB, LANE), jnp.int32)
            kref[...] = jnp.zeros_like(kref)

    for dx, dy in col_sides:

        @pl.when(there(dx, dy))
        def _(dx=dx, dy=dy):
            col_copy(-dx, -dy).wait_recv()

        @pl.when(jnp.logical_not(there(dx, dy)))
        def _(dx=dx, dy=dy):
            if dx == 0:
                colrx[0 if dy < 0 else 1] = jnp.zeros((32, LANE), jnp.float32)
            else:
                cornrx[SIDES.index((dx, dy))] = zero

    for pair in range(4):
        part = pl.ds(8 * pair, 8)
        from_left, from_right = colrx[0, part, :], colrx[1, part, :]
        square[16 * pair : 16 * pair + 8, :] = jnp.where(
            sub < 4, from_left, pltpu.roll(from_right, 4, 0)
        )
        square[16 * pair + 8 : 16 * pair + 16, :] = jnp.where(
            sub < 4, pltpu.roll(from_left, 4, 0), from_right
        )
    upper = lax.rem(lane, 8) < 4
    square[64:72, :] = jnp.where(
        sub < 4,
        jnp.where(upper, cornrx[SIDES.index((-1, -1))], cornrx[SIDES.index((1, -1))]),
        jnp.where(upper, cornrx[SIDES.index((-1, 1))], cornrx[SIDES.index((1, 1))]),
    )

    def steps_of(ref):
        return jnp.broadcast_to(ref[...], (SUB, LANE)).astype(jnp.float32)

    square[72:80, :] = jnp.where(
        sub == 0,
        steps_of(own_k),
        jnp.where(sub == 1, steps_of(up_k), jnp.where(sub == 2, steps_of(down_k), 0.0)),
    )
    square[80:128, :] = jnp.zeros((48, LANE), jnp.float32)
    square[...] = jnp.transpose(square[...])

    halo_lanes = pl.ds(cols, LANE)

    def put_halo(slot, rws, value):
        if slot == LAND:
            rawl[rws, halo_lanes] = value.astype(jnp.int32)
        else:
            raw[slot, rws, halo_lanes] = value

    def unpack(block, carry):
        got = square[pl.ds(pl.multiple_of(block * SUB, SUB), SUB), :]
        rws = pl.ds(pl.multiple_of(SUB + block * SUB, SUB), SUB)
        for slot in range(8):
            put_halo(slot, rws, pltpu.roll(got, LANE - (8 * slot + 4), 1))
        krow[rws, :] = jnp.broadcast_to(got[:, 72:73], (SUB, LANE))
        return carry

    lax.fori_loop(0, blocks, unpack, 0, unroll=4)
    for slot in range(8):
        got = pltpu.roll(square[8 * slot : 8 * slot + 8, :], LANE - 68, 1)
        got = pltpu.roll(got, 4, 0)
        put_halo(slot, pl.ds(0, SUB), got)
        put_halo(slot, pl.ds(rows + SUB, SUB), got)
    krow[0:SUB, :] = jnp.broadcast_to(square[rows - SUB : rows, 73:74], (SUB, LANE))
    krow[rows + SUB : rows + 2 * SUB, :] = jnp.broadcast_to(square[0:SUB, 74:75], (SUB, LANE))

    def prepare_side(block, carry):
        prepare(block, (tiles,))
        return carry

    lax.fori_loop(0, blocks + 2, prepare_side, 0, unroll=6)
    prepare(0, range(tiles))
    prepare(blocks + 1, range(tiles))

    def east(values):
        turned = [pltpu.roll(value, LANE - 1, 1) for value in values]
        return [
            jnp.where(lane == LANE - 1, turned[(tile + 1) % wide], turned[tile])
            for tile in range(wide)
        ]

    def west(values):
        turned = [pltpu.roll(value, 1, 1) for value in values]
        return [
            jnp.where(lane == 0, turned[(tile - 1) % wide], turned[tile])
            for tile in range(wide)
        ]

    def getter(row):
        def get(name, shift=0):
            if shift == 0:
                rws = pl.ds(pl.multiple_of(row, SUB), SUB)
            else:
                rws = pl.ds(row + shift, SUB)
            return [planes[PLANE[name]][tile, rws, :] for tile in range(wide)]

        def put(name, values):
            rws = pl.ds(pl.multiple_of(row, SUB), SUB)
            for tile, value in enumerate(values):
                planes[PLANE[name]][tile, rws, :] = value

        def get_raw(slot):
            rws = pl.ds(pl.multiple_of(row - SUB, SUB), SUB)
            return [raw[slot, rws, tile * LANE : (tile + 1) * LANE] for tile in range(wide)]

        return get, put, get_raw

    def spread(get, name, weights, keep=None, put=None):
        wx, ww, wy, wyn = weights
        here = get(name)
        ahead, behind = east(here), west(here)
        south, north = get(name, 1), get(name, -1)
        fx = [e - c for e, c in zip(ahead, here)]
        fy = [s - c for s, c in zip(south, here)]
        if keep is not None:
            put(keep, fx)
        result = [
            c + ((w * f + v * (b - c)) + (y * g + u * (n - c)))
            for c, w, f, v, b, y, g, u, n in zip(here, wx, fx, ww, behind, wy, fy, wyn, north)
        ]
        return result, fx, fy

    def pass_one(block, carry):
        row = block * SUB
        get, put, get_raw = getter(row)
        rho, lnd = get("rho"), get("lnd")
        rho_e, lnd_e = east(rho), east(lnd)
        wx = [(a + b) * (c * d) for a, b, c, d in zip(rho, rho_e, lnd, lnd_e)]
        rho_s, lnd_s = get("rho", 1), get("lnd", 1)
        wy = [(a + b) * (c * d) for a, b, c, d in zip(rho, rho_s, lnd, lnd_s)]
        rho_n, lnd_n = get("rho", -1), get("lnd", -1)
        wyn = [(a + b) * (c * d) for a, b, c, d in zip(rho, rho_n, lnd, lnd_n)]
        ww = west(wx)
        put("wx", wx)
        put("ww", ww)
        put("wy", wy)
        weights = (wx, ww, wy, wyn)
        ns_, _, _ = spread(get, "n0", weights, "fxn", put)
        qs_, _, _ = spread(get, "q0", weights, "fxq", put)
        ms_, _, _ = spread(get, "m0", weights, "fxm", put)
        z, s0, sel, optimum = get_raw(TRAIT), get("s0"), get("sel"), get_raw(OPT)
        rws = pl.ds(pl.multiple_of(row, SUB), SUB)
        for tile in range(wide):

            def one(name, value, tile=tile):
                planes[PLANE[name]][tile, rws, :] = value

            recip = 1.0 / (ns_[tile] + PRIOR)
            zs = (qs_[tile] + PRIOR * z[tile]) * recip
            ss = (ms_[tile] + PRIOR * s0[tile]) * recip
            vs = ss - zs * zs
            d = zs - optimum[tile]
            growth = lnd[tile] * (
                GROWTH - GROWTH * ns_[tile] - 0.5 * sel[tile] * (d * d + vs)
            )
            grown = jnp.exp(growth)
            n1 = ns_[tile] * grown
            response = sel[tile] * vs
            u = 1.0 / (1.0 + response)
            z1 = zs - response * u * d
            s1 = vs * u + MUTATION + z1 * z1
            one("e1", grown)
            one("r1", recip)
            one("zs1", zs)
            one("ss1", ss)
            one("u1", u)
            one("n1", n1)
            one("z1", z1)
            one("s1", s1)
            one("q1", n1 * z1)
            one("m1", n1 * s1)
        return carry

    def pass_two(block, carry):
        row = block * SUB
        get, put, get_raw = getter(row)
        weights = (get("wx"), get("ww"), get("wy"), get("wy", -1))
        ns_, _, _ = spread(get, "n1", weights, "gxn", put)
        qs_, _, _ = spread(get, "q1", weights, "gxq", put)
        ms_, _, _ = spread(get, "m1", weights, "gxm", put)
        z, s1, sel, lnd = get("z1"), get("s1"), get("sel"), get("lnd")
        optimum, observed = get_raw(OPT), get_raw(OBS)
        rws = pl.ds(pl.multiple_of(row, SUB), SUB)
        chosen = krow[pl.ds(pl.multiple_of(row - SUB, SUB), SUB), :]
        loss = jnp.where(chosen == 2.0, 2.0 * LOSS_WEIGHT, 0.0)
        for tile in range(wide):

            def one(name, value, tile=tile):
                planes[PLANE[name]][tile, rws, :] = value

            recip = 1.0 / (ns_[tile] + PRIOR)
            zs = (qs_[tile] + PRIOR * z[tile]) * recip
            ss = (ms_[tile] + PRIOR * s1[tile]) * recip
            o = optimum[tile]
            phi = ss + o * (o - 2.0 * zs)
            growth = lnd[tile] * (GROWTH - GROWTH * ns_[tile] - 0.5 * sel[tile] * phi)
            grown = jnp.exp(growth)
            n2 = ns_[tile] * grown
            a = (loss * lnd[tile]) * (n2 - observed[tile])
            g = a * n2
            gs = g * sel[tile] * recip
            lq = gs * o
            lm = -0.5 * gs
            one("lq", lq)
            one("lm", lm)
            one("ln", a * grown - 0.5 * g - (zs * lq + ss * lm))
            one("ds", -0.5 * g * phi)
        return carry

    def pass_three(block, carry):
        row = block * SUB
        get, put, get_raw = getter(row)
        weights = (get("wx"), get("ww"), get("wy"), get("wy", -1))
        spreads = []
        gx = gy = None
        for name, state, kept in (("ln", "n1", "gxn"), ("lq", "q1", "gxq"), ("lm", "m1", "gxm")):
            result, fx, fy = spread(get, name, weights)
            spreads.append(result)
            here, south = get(state), get(state, 1)
            px = [a * b for a, b in zip(fx, get(kept))]
            py = [a * (s - c) for a, s, c in zip(fy, south, here)]
            gx = px if gx is None else [a + b for a, b in zip(gx, px)]
            gy = py if gy is None else [a + b for a, b in zip(gy, py)]
        put("gx", gx)
        put("gy", gy)
        mu_n, mu_q, mu_m = spreads
        names = ("n1", "z1", "s1", "e1", "r1", "zs1", "ss1", "u1", "sel", "lnd", "lq", "lm", "ds")
        vals = {name: get(name) for name in names}
        optimum, observed = get_raw(OPT), get_raw(OBS)
        rws = pl.ds(pl.multiple_of(row, SUB), SUB)
        chosen = krow[pl.ds(pl.multiple_of(row - SUB, SUB), SUB), :]
        loss = jnp.where(chosen == 1.0, 2.0 * LOSS_WEIGHT, 0.0)
        for tile in range(wide):

            def one(name, value, tile=tile):
                planes[PLANE[name]][tile, rws, :] = value

            n1, z1, s1, grown, recip, zs, ss, u, sel, lnd, lq, lm, ds = (
                vals[name][tile] for name in names
            )
            c = mu_m[tile] * n1 + PRIOR * lm
            b = mu_q[tile] * n1 + PRIOR * lq + 2.0 * z1 * c
            a = (loss * lnd) * (n1 - observed[tile]) + (
                mu_n[tile] + mu_q[tile] * z1 + mu_m[tile] * s1
            )
            d = zs - optimum[tile]
            vs = ss - zs * zs
            g = a * n1 * lnd
            phi = d * d + vs
            dr = -(u * u) * (b * d + c * vs)
            gs = g * sel
            dd = -(gs * d + b * (1.0 - u))
            dv = c * u + dr * sel - 0.5 * gs
            kq = recip * (b + dd - 2.0 * zs * dv)
            km = recip * dv
            one("kq", kq)
            one("km", km)
            one("kn", a * grown - 0.5 * g - (zs * kq + ss * km))
            one("ds", ds + (dr * vs - 0.5 * g * phi))
        return carry

    def pass_four(block, carry):
        row = block * SUB
        get, put, _ = getter(row)
        gx, gy = get("gx"), get("gy")
        for name, state, kept in (("kn", "n0", "fxn"), ("kq", "q0", "fxq"), ("km", "m0", "fxm")):
            here = get(name)
            fx = get(kept)
            gx = [a + (e - c) * f for a, e, c, f in zip(gx, east(here), here, fx)]
            old = get(state)
            gy = [
                a + (s - c) * (t - o)
                for a, s, c, t, o in zip(gy, get(name, 1), here, get(state, 1), old)
            ]
        lnd, lnd_s = get("lnd"), get("lnd", 1)
        lnd_e = east(lnd)
        hx = [g * (a * b) for g, a, b in zip(gx, lnd, lnd_e)]
        hy = [g * (a * b) for g, a, b in zip(gy, lnd, lnd_s)]
        put("hy", hy)
        total = [a + b + c + d for a, b, c, d in zip(hx, west(hx), hy, get("hy", -1))]
        ds = get("ds")
        rws = pl.ds(pl.multiple_of(row, SUB), SUB)
        for tile in range(tiles):
            gsend[0, tile, rws, :] = -total[tile]
            gsend[1, tile, rws, :] = ds[tile]
        return carry

    def place(owner, piece):
        index = owner * pieces + piece
        return index // tiles, lax.rem(index, tiles)

    def band_rows(band, block, offset):
        return pl.ds(pl.multiple_of(offset + (band * per_band + block) * SUB, SUB), SUB)

    def scatter(band):
        def send(step, carry):
            owner = lax.rem(me_s + step, ns)
            for piece in range(pieces):
                block, tile = place(owner, piece)
                pltpu.make_async_remote_copy(
                    src_ref=gsend.at[:, tile, band_rows(band, block, OFF), :],
                    dst_ref=rrx.at[band, ns - 1 - step, piece],
                    send_sem=rs_send.at[band],
                    recv_sem=rs_recv.at[band],
                    device_id={"scen": owner},
                    device_id_type=MESH,
                ).start()
            return carry

        lax.fori_loop(1, ns, send, 0)

    def all_of(band, sem):
        return pltpu.make_async_copy(rrx.at[band], rrx.at[band], sem.at[band])

    def reduce(band):
        if ns > 1:
            all_of(band, rs_recv).wait()
        for piece in range(pieces):
            block, tile = place(me_s, piece)
            src = band_rows(band, block, OFF)
            for kind in range(2):
                terms = [gsend[kind, tile, src, :]]
                terms += [rrx[band, slot, piece, kind] for slot in range(ns - 1)]
                while len(terms) > 1:
                    pairs = [a + b for a, b in zip(terms[0::2], terms[1::2])]
                    terms = pairs + terms[len(pairs) * 2 :]
                factor = planes[PLANE["fac0"] + kind][tile, src, :]
                total[band, piece, kind] = terms[0] * factor

        def send(step, carry):
            other = lax.rem(me_s + step, ns)
            for piece in range(pieces):
                pltpu.make_async_remote_copy(
                    src_ref=total.at[band, piece],
                    dst_ref=spot(band, piece),
                    send_sem=ag_send.at[band],
                    recv_sem=ag_recv.at[band],
                    device_id={"scen": other},
                    device_id_type=MESH,
                ).start()
            return carry

        lax.fori_loop(1, ns, send, 0)
        for piece in range(pieces):
            own_copy(band, piece).start()

    def spot(band, piece):
        block, tile = place(me_s, piece)
        across = pl.ds(pl.multiple_of(tile * LANE, LANE), LANE)
        return o_grad.at[:, band_rows(band, block, 0), across]

    def own_copy(band, piece):
        return pltpu.make_async_copy(
            total.at[band, piece], spot(band, piece), own_sem.at[band, piece]
        )

    def run(step, start, stop):
        whole = (stop - start) // UNROLL

        def several(count):
            def body(index, carry):
                for part in range(count):
                    step(start + index * UNROLL + part, 0)
                return carry

            return body

        if whole > 0:
            lax.fori_loop(0, whole, several(UNROLL), 0)
        rest = (stop - start) - whole * UNROLL
        if rest > 0:
            several(rest)(jnp.int32(whole), 0)

    last = blocks + 2
    done = [1, 1, 1, 1]
    for band in range(BANDS):
        top_block = 2 + (band + 1) * per_band
        ends = [min(last + 1, top_block + lead) for lead in (3, 2, 1)] + [top_block]
        for index, step in enumerate((pass_one, pass_two, pass_three, pass_four)):
            run(step, done[index], ends[index])
        done = ends
        scatter(band)
        if band >= 1:
            reduce(band - 1)
    reduce(BANDS - 1)

    for dx in (-1, 1):

        @pl.when(there(dx, 0))
        def _(dx=dx):
            for copy in row_copies(dx):
                copy.wait_send()

    for dx, dy in col_sides:

        @pl.when(there(dx, dy))
        def _(dx=dx, dy=dy):
            col_copy(dx, dy).wait_send()

    for band in range(BANDS):
        if ns > 1:
            all_of(band, rs_send).wait()
            all_of(band, ag_send).wait()
            all_of(band, ag_recv).wait()
        for piece in range(pieces):
            own_copy(band, piece).wait()


def solution(mesh):
    ns, nx, ny = (mesh.shape[name] for name in ("scen", "lx", "ly"))

    def shards(density, trait, variance, optimum, observed, obs_step, land_code, maps, first, second):
        _, rows, cols = density.shape
        tiles = cols // LANE
        per_band = rows // SUB // BANDS
        pieces = per_band * tiles // ns
        f32 = jnp.float32
        shape = jax.ShapeDtypeStruct(maps.shape, f32)
        dma = pltpu.SemaphoreType.DMA
        gradient = pl.pallas_call(
            functools.partial(kernel, (ns, nx, ny, rows, cols)),
            out_shape=shape,
            in_specs=[pl.BlockSpec(memory_space=pltpu.HBM)] * 8,
            out_specs=pl.BlockSpec(memory_space=pl.ANY),
            scratch_shapes=[
                pltpu.VMEM((7, rows + 2 * SUB, cols + LANE), f32),
                pltpu.VMEM((rows + 2 * SUB, cols + LANE), jnp.int32),
                pltpu.VMEM((1, rows), jnp.int32),
                pltpu.VMEM((1, rows), jnp.int32),
                pltpu.VMEM((1, rows), jnp.int32),
                pltpu.VMEM((rows + 2 * SUB, LANE), f32),
                pltpu.VMEM((2, 32, LANE), f32),
                pltpu.VMEM((SUB, LANE), f32),
                pltpu.VMEM((2, 32, LANE), f32),
                pltpu.VMEM((8, SUB, LANE), f32),
                pltpu.VMEM((LANE, LANE), f32),
                pltpu.VMEM((2, tiles, rows + 2 * OFF, LANE), f32),
                pltpu.VMEM((BANDS, max(ns - 1, 1), pieces, 2, SUB, LANE), f32),
                pltpu.VMEM((BANDS, pieces, 2, SUB, LANE), f32),
                dma((9,)),
                dma((2, 8)),
                dma((2, 8)),
                dma((8,)),
                dma((8,)),
                dma((BANDS,)),
                dma((BANDS,)),
                dma((BANDS,)),
                dma((BANDS,)),
                dma((BANDS, pieces)),
            ]
            + [pltpu.VMEM((tiles + 1, rows + 2 * OFF, LANE), f32)] * len(NAMES),
            compiler_params=pltpu.CompilerParams(
                collective_id=0, has_side_effects=True, vmem_limit_bytes=60 * 1024 * 1024
            ),
        )(density, trait, variance, optimum, observed, obs_step, land_code, maps)
        new_first = BETA_FIRST * first + (1.0 - BETA_FIRST) * gradient
        new_second = BETA_SECOND * second + (1.0 - BETA_SECOND) * gradient * gradient
        first_hat = new_first / (1.0 - BETA_FIRST**ADAM_STEP)
        second_hat = new_second / (1.0 - BETA_SECOND**ADAM_STEP)
        new_maps = maps - LEARN_RATE * first_hat / (jnp.sqrt(second_hat) + ADAM_EPS)
        return new_maps, new_first, new_second

    tile = P("scen", "lx", "ly")
    flat = P(None, "lx", "ly")
    return jax.shard_map(
        shards,
        mesh=mesh,
        in_specs=(tile,) * 5 + (P("scen", "lx"), P("lx", "ly"), flat, flat, flat),
        out_specs=(flat, flat, flat),
        check_vma=False,
    )
```

```python
import functools

import jax
import jax.numpy as jnp
from jax import lax
from jax.experimental import pallas as pl
from jax.experimental.pallas import tpu as pltpu
from jax.sharding import PartitionSpec as P

ADAM_STEP = 10
REACH_MAX = 0.2
PRIOR = 0.1
GROWTH = 0.5
MUTATION = 0.02
LEARN_RATE = 0.01
BETA_FIRST = 0.9
BETA_SECOND = 0.999
ADAM_EPS = 1e-08
LOSS_WEIGHT = 2.0

MESH = pl.DeviceIdType.MESH
SUB, LANE = 8, 128
HALO = 4
BANDS = 4
UNROLL = 4
OFF = 16
DENS, TRAIT, VAR, OPT, OBS, MAP0, MAP1, LAND = range(8)
SIDES = [(-1, -1), (-1, 0), (-1, 1), (0, -1), (0, 1), (1, -1), (1, 0), (1, 1)]
NAMES = (
    "n0", "q0", "m0", "s0", "rho", "lnd", "sel", "wx",
    "ww", "wy", "n1", "q1", "m1", "z1", "s1", "e1", "r1",
    "zs1", "ss1", "u1", "fxn", "fxq", "fxm", "gxn", "gxq",
    "gxm", "ln", "lq", "lm", "kn", "kq", "km", "ds",
    "gx", "gy", "hy", "fac0", "fac1",
)
PLANE = {name: index for index, name in enumerate(NAMES)}


def kernel(
    sizes,
    dens,
    trait,
    var,
    opt,
    obs,
    ostep,
    land,
    maps,
    o_grad,
    raw,
    rawl,
    own_k,
    up_k,
    down_k,
    krow,
    colsend,
    cornsend,
    colrx,
    cornrx,
    square,
    gsend,
    rrx,
    total,
    load_sem,
    row_send,
    row_recv,
    col_send,
    col_recv,
    rs_send,
    rs_recv,
    ag_send,
    ag_recv,
    own_sem,
    *planes,
):
    ns, nx, ny, rows, cols = sizes
    tiles = cols // LANE
    wide = tiles + 1
    blocks = rows // SUB
    per_band = blocks // BANDS
    pieces = per_band * tiles // ns
    me_s, me_x, me_y = (lax.axis_index(name) for name in ("scen", "lx", "ly"))
    top, bottom = me_x == 0, me_x == nx - 1
    left, right = me_y == 0, me_y == ny - 1
    lane = lax.broadcasted_iota(jnp.int32, (SUB, LANE), 1)
    sub = lax.broadcasted_iota(jnp.int32, (SUB, LANE), 0)

    def there(dx, dy):
        ok = jnp.bool_(True)
        if dx:
            ok = jnp.logical_not(top if dx < 0 else bottom)
        if dy:
            oky = jnp.logical_not(left if dy < 0 else right)
            ok = jnp.logical_and(ok, oky) if dx else oky
        return ok

    def target(dx, dy):
        return {"lx": me_x + dx, "ly": me_y + dy}

    body = pl.ds(SUB, rows)
    loads = []
    for slot, ref in enumerate((dens, trait, var, opt, obs)):
        loads.append((ref.at[0], raw.at[slot, body, pl.ds(0, cols)]))
    for slot in range(2):
        loads.append((maps.at[slot], raw.at[MAP0 + slot, body, pl.ds(0, cols)]))
    loads.append((land, rawl.at[body, pl.ds(0, cols)]))
    loads.append((ostep, own_k))
    loads = [
        pltpu.make_async_copy(src, dst, load_sem.at[slot])
        for slot, (src, dst) in enumerate(loads)
    ]
    for copy in loads:
        copy.start()

    barrier = pltpu.get_barrier_semaphore()

    def greet(step, carry):
        pl.semaphore_signal(
            barrier, inc=1, device_id={"scen": lax.rem(me_s + step, ns)}, device_id_type=MESH
        )
        return carry

    lax.fori_loop(1, ns, greet, 0)
    for dx, dy in SIDES:

        @pl.when(there(dx, dy))
        def _(dx=dx, dy=dy):
            pl.semaphore_signal(barrier, inc=1, device_id=target(dx, dy), device_id_type=MESH)

    over_x = jnp.where(top, 0, 1) + jnp.where(bottom, 0, 1)
    over_y = jnp.where(left, 0, 1) + jnp.where(right, 0, 1)

    def row_copies(dx):
        edge = pl.ds(0, HALO) if dx < 0 else pl.ds(rows - HALO, HALO)
        halo = pl.ds(rows + SUB, HALO) if dx < 0 else pl.ds(SUB - HALO, HALO)
        across = pl.ds(0, cols)
        pairs = [
            (ref.at[0, edge, :], raw.at[slot, halo, across])
            for slot, ref in enumerate((dens, trait, var, opt, obs))
        ]
        pairs.append((maps.at[:, edge, :], raw.at[pl.ds(MAP0, 2), halo, across]))
        pairs.append((land.at[edge, :], rawl.at[halo, across]))
        pairs.append((ostep, down_k if dx < 0 else up_k))
        way = 0 if dx < 0 else 1
        return [
            pltpu.make_async_remote_copy(
                src_ref=src,
                dst_ref=dst,
                send_sem=row_send.at[way, slot],
                recv_sem=row_recv.at[way, slot],
                device_id=target(dx, 0),
                device_id_type=MESH,
            )
            for slot, (src, dst) in enumerate(pairs)
        ]

    for copy in loads:
        copy.wait()

    def field(slot, rws, cls):
        if slot == LAND:
            return rawl[rws, cls].astype(jnp.float32)
        return raw[slot, rws, cls]

    def pack(block, carry):
        rws = pl.ds(pl.multiple_of(SUB + block * SUB, SUB), SUB)
        packed = jnp.zeros((SUB, LANE), jnp.float32)
        for slot in range(8):
            pair = jnp.where(
                lane < LANE // 2,
                field(slot, rws, pl.ds(0, LANE)),
                field(slot, rws, pl.ds(cols - LANE, LANE)),
            )
            turned = pltpu.roll(pair, 8 * slot + 4, 1)
            packed = jnp.where(lane // 8 == slot, turned, packed)
        square[pl.ds(pl.multiple_of(block * SUB, SUB), SUB), :] = packed
        return carry

    lax.fori_loop(0, blocks, pack, 0, unroll=4)
    turned = jnp.transpose(square[...])
    corner = jnp.zeros((SUB, LANE), jnp.float32)
    for slot in range(8):
        part = turned[8 * slot : 8 * slot + 8, :]
        corner = jnp.where(lane // 8 == slot, pltpu.roll(part, 8 * slot + 4, 1), corner)
    for pair in range(4):
        even = turned[16 * pair : 16 * pair + 8, :]
        odd = turned[16 * pair + 8 : 16 * pair + 16, :]
        colsend[0, 8 * pair : 8 * pair + 8, :] = jnp.where(sub < 4, even, pltpu.roll(odd, 4, 0))
        colsend[1, 8 * pair : 8 * pair + 8, :] = jnp.where(sub < 4, pltpu.roll(even, 4, 0), odd)
    cornsend[...] = corner

    def prepare(block, lanes):
        src = pl.ds(pl.multiple_of(block * SUB, SUB), SUB)
        dst = pl.ds(pl.multiple_of(block * SUB + OFF - SUB, SUB), SUB)
        for tile in lanes:
            cls = pl.ds(tile * LANE, LANE)
            n, z, v = raw[DENS, src, cls], raw[TRAIT, src, cls], raw[VAR, src, cls]
            second_moment = v + z * z

            def put(name, value):
                planes[PLANE[name]][tile, dst, :] = value

            put("n0", n)
            put("q0", n * z)
            put("s0", second_moment)
            put("m0", n * second_moment)
            put("lnd", rawl[src, cls].astype(jnp.float32))
            share = 1.0 / (1.0 + jnp.exp(-raw[MAP0, src, cls]))
            rho = (0.5 * REACH_MAX) * share
            put("rho", rho)
            x = raw[MAP1, src, cls]
            small = jnp.exp(-jnp.abs(x))
            put("sel", jnp.maximum(x, 0.0) + jnp.log1p(small))
            if tile < tiles:
                put("fac0", rho * (1.0 - share))
                put("fac1", jnp.where(x >= 0.0, 1.0, small) / (1.0 + small))

    def prepare_own(block, carry):
        prepare(block, range(tiles))
        return carry


    pl.semaphore_wait(barrier, ns - 1 + (over_x + 1) * (over_y + 1) - 1)
    def col_copy(dx, dy):
        index = SIDES.index((dx, dy))
        came = SIDES.index((-dx, -dy))
        if dx == 0:
            way = 0 if dy > 0 else 1
            src, dst = colsend.at[way], colrx.at[way]
        else:
            src, dst = cornsend, cornrx.at[came]
        return pltpu.make_async_remote_copy(
            src_ref=src,
            dst_ref=dst,
            send_sem=col_send.at[index],
            recv_sem=col_recv.at[came],
            device_id=target(dx, dy),
            device_id_type=MESH,
        )

    col_sides = [side for side in SIDES if side[1]]
    for dx, dy in col_sides:

        @pl.when(there(dx, dy))
        def _(dx=dx, dy=dy):
            col_copy(dx, dy).start()

    for dx in (-1, 1):

        @pl.when(there(dx, 0))
        def _(dx=dx):
            for copy in row_copies(dx):
                copy.start()

    lax.fori_loop(1, blocks + 1, prepare_own, 0, unroll=4)

    soon = min(blocks, 2 * per_band)
    zero = jnp.zeros((SUB, LANE), jnp.float32)
    for dx, halo, kref in ((-1, 0, up_k), (1, rows + SUB, down_k)):

        @pl.when(there(dx, 0))
        def _(dx=dx):
            for copy in row_copies(-dx):
                copy.wait_recv()

        @pl.when(jnp.logical_not(there(dx, 0)))
        def _(halo=halo, kref=kref):
            for tile in range(tiles):
                cls = pl.ds(tile * LANE, LANE)
                for slot in range(7):
                    raw[slot, pl.ds(halo, SUB), cls] = zero
                rawl[pl.ds(halo, SUB), cls] = jnp.zeros((SUB, LANE), jnp.int32)
            kref[...] = jnp.zeros_like(kref)

    for dx, dy in col_sides:

        @pl.when(there(dx, dy))
        def _(dx=dx, dy=dy):
            col_copy(-dx, -dy).wait_recv()

        @pl.when(jnp.logical_not(there(dx, dy)))
        def _(dx=dx, dy=dy):
            if dx == 0:
                colrx[0 if dy < 0 else 1] = jnp.zeros((32, LANE), jnp.float32)
            else:
                cornrx[SIDES.index((dx, dy))] = zero

    for pair in range(4):
        part = pl.ds(8 * pair, 8)
        from_left, from_right = colrx[0, part, :], colrx[1, part, :]
        square[16 * pair : 16 * pair + 8, :] = jnp.where(
            sub < 4, from_left, pltpu.roll(from_right, 4, 0)
        )
        square[16 * pair + 8 : 16 * pair + 16, :] = jnp.where(
            sub < 4, pltpu.roll(from_left, 4, 0), from_right
        )
    upper = lax.rem(lane, 8) < 4
    square[64:72, :] = jnp.where(
        sub < 4,
        jnp.where(upper, cornrx[SIDES.index((-1, -1))], cornrx[SIDES.index((1, -1))]),
        jnp.where(upper, cornrx[SIDES.index((-1, 1))], cornrx[SIDES.index((1, 1))]),
    )

    def steps_of(ref):
        return jnp.broadcast_to(ref[...], (SUB, LANE)).astype(jnp.float32)

    square[72:80, :] = jnp.where(
        sub == 0,
        steps_of(own_k),
        jnp.where(sub == 1, steps_of(up_k), jnp.where(sub == 2, steps_of(down_k), 0.0)),
    )
    square[80:128, :] = jnp.zeros((48, LANE), jnp.float32)
    square[...] = jnp.transpose(square[...])

    halo_lanes = pl.ds(cols, LANE)

    def put_halo(slot, rws, value):
        if slot == LAND:
            rawl[rws, halo_lanes] = value.astype(jnp.int32)
        else:
            raw[slot, rws, halo_lanes] = value

    def unpack(block, carry):
        got = square[pl.ds(pl.multiple_of(block * SUB, SUB), SUB), :]
        rws = pl.ds(pl.multiple_of(SUB + block * SUB, SUB), SUB)
        for slot in range(8):
            put_halo(slot, rws, pltpu.roll(got, LANE - (8 * slot + 4), 1))
        krow[rws, :] = jnp.broadcast_to(got[:, 72:73], (SUB, LANE))
        return carry

    lax.fori_loop(0, soon, unpack, 0, unroll=4)
    for slot in range(8):
        got = pltpu.roll(square[8 * slot : 8 * slot + 8, :], LANE - 68, 1)
        got = pltpu.roll(got, 4, 0)
        put_halo(slot, pl.ds(0, SUB), got)
        put_halo(slot, pl.ds(rows + SUB, SUB), got)
    krow[0:SUB, :] = jnp.broadcast_to(square[rows - SUB : rows, 73:74], (SUB, LANE))
    krow[rows + SUB : rows + 2 * SUB, :] = jnp.broadcast_to(square[0:SUB, 74:75], (SUB, LANE))

    def prepare_side(block, carry):
        prepare(block, (tiles,))
        return carry

    lax.fori_loop(0, soon + 1, prepare_side, 0, unroll=3)
    prepare(0, range(tiles))

    def finish_halo():
        lax.fori_loop(soon, blocks, unpack, 0, unroll=4)
        lax.fori_loop(soon + 1, blocks + 2, prepare_side, 0, unroll=3)
        prepare(blocks + 1, range(tiles))


    def east(values):
        turned = [pltpu.roll(value, LANE - 1, 1) for value in values]
        return [
            jnp.where(lane == LANE - 1, turned[(tile + 1) % wide], turned[tile])
            for tile in range(wide)
        ]

    def west(values):
        turned = [pltpu.roll(value, 1, 1) for value in values]
        return [
            jnp.where(lane == 0, turned[(tile - 1) % wide], turned[tile])
            for tile in range(wide)
        ]

    def getter(row):
        def get(name, shift=0):
            if shift == 0:
                rws = pl.ds(pl.multiple_of(row, SUB), SUB)
            else:
                rws = pl.ds(row + shift, SUB)
            return [planes[PLANE[name]][tile, rws, :] for tile in range(wide)]

        def put(name, values):
            rws = pl.ds(pl.multiple_of(row, SUB), SUB)
            for tile, value in enumerate(values):
                planes[PLANE[name]][tile, rws, :] = value

        def get_raw(slot):
            rws = pl.ds(pl.multiple_of(row - SUB, SUB), SUB)
            return [raw[slot, rws, tile * LANE : (tile + 1) * LANE] for tile in range(wide)]

        return get, put, get_raw

    def spread(get, name, weights, keep=None, put=None):
        wx, ww, wy, wyn = weights
        here = get(name)
        ahead, behind = east(here), west(here)
        south, north = get(name, 1), get(name, -1)
        fx = [e - c for e, c in zip(ahead, here)]
        fy = [s - c for s, c in zip(south, here)]
        if keep is not None:
            put(keep, fx)
        result = [
            c + ((w * f + v * (b - c)) + (y * g + u * (n - c)))
            for c, w, f, v, b, y, g, u, n in zip(here, wx, fx, ww, behind, wy, fy, wyn, north)
        ]
        return result, fx, fy

    def pass_one(block, carry):
        row = block * SUB
        get, put, get_raw = getter(row)
        rho, lnd = get("rho"), get("lnd")
        rho_e, lnd_e = east(rho), east(lnd)
        wx = [(a + b) * (c * d) for a, b, c, d in zip(rho, rho_e, lnd, lnd_e)]
        rho_s, lnd_s = get("rho", 1), get("lnd", 1)
        wy = [(a + b) * (c * d) for a, b, c, d in zip(rho, rho_s, lnd, lnd_s)]
        rho_n, lnd_n = get("rho", -1), get("lnd", -1)
        wyn = [(a + b) * (c * d) for a, b, c, d in zip(rho, rho_n, lnd, lnd_n)]
        ww = west(wx)
        put("wx", wx)
        put("ww", ww)
        put("wy", wy)
        weights = (wx, ww, wy, wyn)
        ns_, _, _ = spread(get, "n0", weights, "fxn", put)
        qs_, _, _ = spread(get, "q0", weights, "fxq", put)
        ms_, _, _ = spread(get, "m0", weights, "fxm", put)
        z, s0, sel, optimum = get_raw(TRAIT), get("s0"), get("sel"), get_raw(OPT)
        rws = pl.ds(pl.multiple_of(row, SUB), SUB)
        for tile in range(wide):

            def one(name, value, tile=tile):
                planes[PLANE[name]][tile, rws, :] = value

            recip = 1.0 / (ns_[tile] + PRIOR)
            zs = (qs_[tile] + PRIOR * z[tile]) * recip
            ss = (ms_[tile] + PRIOR * s0[tile]) * recip
            vs = ss - zs * zs
            d = zs - optimum[tile]
            growth = lnd[tile] * (
                GROWTH - GROWTH * ns_[tile] - 0.5 * sel[tile] * (d * d + vs)
            )
            grown = jnp.exp(growth)
            n1 = ns_[tile] * grown
            response = sel[tile] * vs
            u = 1.0 / (1.0 + response)
            z1 = zs - response * u * d
            s1 = vs * u + MUTATION + z1 * z1
            one("e1", grown)
            one("r1", recip)
            one("zs1", zs)
            one("ss1", ss)
            one("u1", u)
            one("n1", n1)
            one("z1", z1)
            one("s1", s1)
            one("q1", n1 * z1)
            one("m1", n1 * s1)
        return carry

    def pass_two(block, carry):
        row = block * SUB
        get, put, get_raw = getter(row)
        weights = (get("wx"), get("ww"), get("wy"), get("wy", -1))
        ns_, _, _ = spread(get, "n1", weights, "gxn", put)
        qs_, _, _ = spread(get, "q1", weights, "gxq", put)
        ms_, _, _ = spread(get, "m1", weights, "gxm", put)
        z, s1, sel, lnd = get("z1"), get("s1"), get("sel"), get("lnd")
        optimum, observed = get_raw(OPT), get_raw(OBS)
        rws = pl.ds(pl.multiple_of(row, SUB), SUB)
        chosen = krow[pl.ds(pl.multiple_of(row - SUB, SUB), SUB), :]
        loss = jnp.where(chosen == 2.0, 2.0 * LOSS_WEIGHT, 0.0)
        for tile in range(wide):

            def one(name, value, tile=tile):
                planes[PLANE[name]][tile, rws, :] = value

            recip = 1.0 / (ns_[tile] + PRIOR)
            zs = (qs_[tile] + PRIOR * z[tile]) * recip
            ss = (ms_[tile] + PRIOR * s1[tile]) * recip
            o = optimum[tile]
            phi = ss + o * (o - 2.0 * zs)
            growth = lnd[tile] * (GROWTH - GROWTH * ns_[tile] - 0.5 * sel[tile] * phi)
            grown = jnp.exp(growth)
            n2 = ns_[tile] * grown
            a = (loss * lnd[tile]) * (n2 - observed[tile])
            g = a * n2
            gs = g * sel[tile] * recip
            lq = gs * o
            lm = -0.5 * gs
            one("lq", lq)
            one("lm", lm)
            one("ln", a * grown - 0.5 * g - (zs * lq + ss * lm))
            one("ds", -0.5 * g * phi)
        return carry

    def pass_three(block, carry):
        row = block * SUB
        get, put, get_raw = getter(row)
        weights = (get("wx"), get("ww"), get("wy"), get("wy", -1))
        spreads = []
        gx = gy = None
        for name, state, kept in (("ln", "n1", "gxn"), ("lq", "q1", "gxq"), ("lm", "m1", "gxm")):
            result, fx, fy = spread(get, name, weights)
            spreads.append(result)
            here, south = get(state), get(state, 1)
            px = [a * b for a, b in zip(fx, get(kept))]
            py = [a * (s - c) for a, s, c in zip(fy, south, here)]
            gx = px if gx is None else [a + b for a, b in zip(gx, px)]
            gy = py if gy is None else [a + b for a, b in zip(gy, py)]
        put("gx", gx)
        put("gy", gy)
        mu_n, mu_q, mu_m = spreads
        names = ("n1", "z1", "s1", "e1", "r1", "zs1", "ss1", "u1", "sel", "lnd", "lq", "lm", "ds")
        vals = {name: get(name) for name in names}
        optimum, observed = get_raw(OPT), get_raw(OBS)
        rws = pl.ds(pl.multiple_of(row, SUB), SUB)
        chosen = krow[pl.ds(pl.multiple_of(row - SUB, SUB), SUB), :]
        loss = jnp.where(chosen == 1.0, 2.0 * LOSS_WEIGHT, 0.0)
        for tile in range(wide):

            def one(name, value, tile=tile):
                planes[PLANE[name]][tile, rws, :] = value

            n1, z1, s1, grown, recip, zs, ss, u, sel, lnd, lq, lm, ds = (
                vals[name][tile] for name in names
            )
            c = mu_m[tile] * n1 + PRIOR * lm
            b = mu_q[tile] * n1 + PRIOR * lq + 2.0 * z1 * c
            a = (loss * lnd) * (n1 - observed[tile]) + (
                mu_n[tile] + mu_q[tile] * z1 + mu_m[tile] * s1
            )
            d = zs - optimum[tile]
            vs = ss - zs * zs
            g = a * n1 * lnd
            phi = d * d + vs
            dr = -(u * u) * (b * d + c * vs)
            gs = g * sel
            dd = -(gs * d + b * (1.0 - u))
            dv = c * u + dr * sel - 0.5 * gs
            kq = recip * (b + dd - 2.0 * zs * dv)
            km = recip * dv
            one("kq", kq)
            one("km", km)
            one("kn", a * grown - 0.5 * g - (zs * kq + ss * km))
            one("ds", ds + (dr * vs - 0.5 * g * phi))
        return carry

    def pass_four(block, carry):
        row = block * SUB
        get, put, _ = getter(row)
        gx, gy = get("gx"), get("gy")
        for name, state, kept in (("kn", "n0", "fxn"), ("kq", "q0", "fxq"), ("km", "m0", "fxm")):
            here = get(name)
            fx = get(kept)
            gx = [a + (e - c) * f for a, e, c, f in zip(gx, east(here), here, fx)]
            old = get(state)
            gy = [
                a + (s - c) * (t - o)
                for a, s, c, t, o in zip(gy, get(name, 1), here, get(state, 1), old)
            ]
        lnd, lnd_s = get("lnd"), get("lnd", 1)
        lnd_e = east(lnd)
        hx = [g * (a * b) for g, a, b in zip(gx, lnd, lnd_e)]
        hy = [g * (a * b) for g, a, b in zip(gy, lnd, lnd_s)]
        put("hy", hy)
        total = [a + b + c + d for a, b, c, d in zip(hx, west(hx), hy, get("hy", -1))]
        ds = get("ds")
        rws = pl.ds(pl.multiple_of(row, SUB), SUB)
        for tile in range(tiles):
            gsend[0, tile, rws, :] = -total[tile]
            gsend[1, tile, rws, :] = ds[tile]
        return carry

    def place(owner, piece):
        index = owner * pieces + piece
        return index // tiles, lax.rem(index, tiles)

    def band_rows(band, block, offset):
        return pl.ds(pl.multiple_of(offset + (band * per_band + block) * SUB, SUB), SUB)

    def scatter(band):
        def send(step, carry):
            owner = lax.rem(me_s + step, ns)
            for piece in range(pieces):
                block, tile = place(owner, piece)
                pltpu.make_async_remote_copy(
                    src_ref=gsend.at[:, tile, band_rows(band, block, OFF), :],
                    dst_ref=rrx.at[band, ns - 1 - step, piece],
                    send_sem=rs_send.at[band],
                    recv_sem=rs_recv.at[band],
                    device_id={"scen": owner},
                    device_id_type=MESH,
                ).start()
            return carry

        lax.fori_loop(1, ns, send, 0)

    def all_of(band, sem):
        return pltpu.make_async_copy(rrx.at[band], rrx.at[band], sem.at[band])

    def reduce(band):
        if ns > 1:
            all_of(band, rs_recv).wait()
        for piece in range(pieces):
            block, tile = place(me_s, piece)
            src = band_rows(band, block, OFF)
            for kind in range(2):
                terms = [gsend[kind, tile, src, :]]
                terms += [rrx[band, slot, piece, kind] for slot in range(ns - 1)]
                while len(terms) > 1:
                    pairs = [a + b for a, b in zip(terms[0::2], terms[1::2])]
                    terms = pairs + terms[len(pairs) * 2 :]
                factor = planes[PLANE["fac0"] + kind][tile, src, :]
                total[band, piece, kind] = terms[0] * factor

        def send(step, carry):
            other = lax.rem(me_s + step, ns)
            for piece in range(pieces):
                pltpu.make_async_remote_copy(
                    src_ref=total.at[band, piece],
                    dst_ref=spot(band, piece),
                    send_sem=ag_send.at[band],
                    recv_sem=ag_recv.at[band],
                    device_id={"scen": other},
                    device_id_type=MESH,
                ).start()
            return carry

        lax.fori_loop(1, ns, send, 0)
        for piece in range(pieces):
            own_copy(band, piece).start()

    def spot(band, piece):
        block, tile = place(me_s, piece)
        across = pl.ds(pl.multiple_of(tile * LANE, LANE), LANE)
        return o_grad.at[:, band_rows(band, block, 0), across]

    def own_copy(band, piece):
        return pltpu.make_async_copy(
            total.at[band, piece], spot(band, piece), own_sem.at[band, piece]
        )

    def run(step, start, stop):
        whole = (stop - start) // UNROLL

        def several(count):
            def body(index, carry):
                for part in range(count):
                    step(start + index * UNROLL + part, 0)
                return carry

            return body

        if whole > 0:
            lax.fori_loop(0, whole, several(UNROLL), 0)
        rest = (stop - start) - whole * UNROLL
        if rest > 0:
            several(rest)(jnp.int32(whole), 0)

    last = blocks + 2
    done = [1, 1, 1, 1]
    for band in range(BANDS):
        top_block = 2 + (band + 1) * per_band
        ends = [min(last + 1, top_block + lead) for lead in (3, 2, 1)] + [top_block]
        for index, step in enumerate((pass_one, pass_two, pass_three, pass_four)):
            run(step, done[index], ends[index])
        done = ends
        scatter(band)
        if band == 0:
            finish_halo()
        if band >= 1:
            reduce(band - 1)
    reduce(BANDS - 1)

    for dx in (-1, 1):

        @pl.when(there(dx, 0))
        def _(dx=dx):
            for copy in row_copies(dx):
                copy.wait_send()

    for dx, dy in col_sides:

        @pl.when(there(dx, dy))
        def _(dx=dx, dy=dy):
            col_copy(dx, dy).wait_send()

    for band in range(BANDS):
        if ns > 1:
            all_of(band, rs_send).wait()
            all_of(band, ag_send).wait()
            all_of(band, ag_recv).wait()
        for piece in range(pieces):
            own_copy(band, piece).wait()


def solution(mesh):
    ns, nx, ny = (mesh.shape[name] for name in ("scen", "lx", "ly"))

    def shards(density, trait, variance, optimum, observed, obs_step, land_code, maps, first, second):
        _, rows, cols = density.shape
        tiles = cols // LANE
        per_band = rows // SUB // BANDS
        pieces = per_band * tiles // ns
        f32 = jnp.float32
        shape = jax.ShapeDtypeStruct(maps.shape, f32)
        dma = pltpu.SemaphoreType.DMA
        gradient = pl.pallas_call(
            functools.partial(kernel, (ns, nx, ny, rows, cols)),
            out_shape=shape,
            in_specs=[pl.BlockSpec(memory_space=pltpu.HBM)] * 8,
            out_specs=pl.BlockSpec(memory_space=pl.ANY),
            scratch_shapes=[
                pltpu.VMEM((7, rows + 2 * SUB, cols + LANE), f32),
                pltpu.VMEM((rows + 2 * SUB, cols + LANE), jnp.int32),
                pltpu.VMEM((1, rows), jnp.int32),
                pltpu.VMEM((1, rows), jnp.int32),
                pltpu.VMEM((1, rows), jnp.int32),
                pltpu.VMEM((rows + 2 * SUB, LANE), f32),
                pltpu.VMEM((2, 32, LANE), f32),
                pltpu.VMEM((SUB, LANE), f32),
                pltpu.VMEM((2, 32, LANE), f32),
                pltpu.VMEM((8, SUB, LANE), f32),
                pltpu.VMEM((LANE, LANE), f32),
                pltpu.VMEM((2, tiles, rows + 2 * OFF, LANE), f32),
                pltpu.VMEM((BANDS, max(ns - 1, 1), pieces, 2, SUB, LANE), f32),
                pltpu.VMEM((BANDS, pieces, 2, SUB, LANE), f32),
                dma((9,)),
                dma((2, 8)),
                dma((2, 8)),
                dma((8,)),
                dma((8,)),
                dma((BANDS,)),
                dma((BANDS,)),
                dma((BANDS,)),
                dma((BANDS,)),
                dma((BANDS, pieces)),
            ]
            + [pltpu.VMEM((tiles + 1, rows + 2 * OFF, LANE), f32)] * len(NAMES),
            compiler_params=pltpu.CompilerParams(
                collective_id=0, has_side_effects=True, vmem_limit_bytes=60 * 1024 * 1024
            ),
        )(density, trait, variance, optimum, observed, obs_step, land_code, maps)
        new_first = BETA_FIRST * first + (1.0 - BETA_FIRST) * gradient
        new_second = BETA_SECOND * second + (1.0 - BETA_SECOND) * gradient * gradient
        first_hat = new_first / (1.0 - BETA_FIRST**ADAM_STEP)
        second_hat = new_second / (1.0 - BETA_SECOND**ADAM_STEP)
        new_maps = maps - LEARN_RATE * first_hat / (jnp.sqrt(second_hat) + ADAM_EPS)
        return new_maps, new_first, new_second

    tile = P("scen", "lx", "ly")
    flat = P(None, "lx", "ly")
    return jax.shard_map(
        shards,
        mesh=mesh,
        in_specs=(tile,) * 5 + (P("scen", "lx"), P("lx", "ly"), flat, flat, flat),
        out_specs=(flat, flat, flat),
        check_vma=False,
    )
```

```python
import functools

import jax
import jax.numpy as jnp
from jax import lax
from jax.experimental import pallas as pl
from jax.experimental.pallas import tpu as pltpu
from jax.sharding import PartitionSpec as P

ADAM_STEP = 10
REACH_MAX = 0.2
PRIOR = 0.1
GROWTH = 0.5
MUTATION = 0.02
LEARN_RATE = 0.01
BETA_FIRST = 0.9
BETA_SECOND = 0.999
ADAM_EPS = 1e-08
LOSS_WEIGHT = 2.0

MESH = pl.DeviceIdType.MESH
SUB, LANE = 8, 128
HALO = 4
BANDS = 4
UNROLL = 4
OFF = 16
DENS, TRAIT, VAR, OPT, OBS, MAP0, MAP1, LAND = range(8)
SIDES = [(-1, -1), (-1, 0), (-1, 1), (0, -1), (0, 1), (1, -1), (1, 0), (1, 1)]
NAMES = (
    "n0", "q0", "m0", "s0", "rho", "lnd", "sel", "wx",
    "ww", "wy", "n1", "q1", "m1", "z1", "s1", "e1", "r1",
    "zs1", "ss1", "u1", "fxn", "fxq", "fxm", "gxn", "gxq",
    "gxm", "ln", "lq", "lm", "kn", "kq", "km", "ds",
    "gx", "gy", "hy", "fac0", "fac1",
)
PLANE = {name: index for index, name in enumerate(NAMES)}


def kernel(
    sizes,
    dens,
    trait,
    var,
    opt,
    obs,
    ostep,
    land,
    maps,
    o_grad,
    raw,
    rawl,
    own_k,
    up_k,
    down_k,
    krow,
    colsend,
    cornsend,
    colrx,
    cornrx,
    square,
    gsend,
    rrx,
    total,
    load_sem,
    row_send,
    row_recv,
    col_send,
    col_recv,
    rs_send,
    rs_recv,
    ag_send,
    ag_recv,
    own_sem,
    *planes,
):
    ns, nx, ny, rows, cols = sizes
    tiles = cols // LANE
    wide = tiles + 1
    blocks = rows // SUB
    per_band = blocks // BANDS
    pieces = per_band * tiles // ns
    me_s, me_x, me_y = (lax.axis_index(name) for name in ("scen", "lx", "ly"))
    top, bottom = me_x == 0, me_x == nx - 1
    left, right = me_y == 0, me_y == ny - 1
    lane = lax.broadcasted_iota(jnp.int32, (SUB, LANE), 1)
    sub = lax.broadcasted_iota(jnp.int32, (SUB, LANE), 0)

    def there(dx, dy):
        ok = jnp.bool_(True)
        if dx:
            ok = jnp.logical_not(top if dx < 0 else bottom)
        if dy:
            oky = jnp.logical_not(left if dy < 0 else right)
            ok = jnp.logical_and(ok, oky) if dx else oky
        return ok

    def target(dx, dy):
        return {"lx": me_x + dx, "ly": me_y + dy}

    body = pl.ds(SUB, rows)
    loads = []
    for slot, ref in enumerate((dens, trait, var, opt, obs)):
        loads.append((ref.at[0], raw.at[slot, body, pl.ds(0, cols)]))
    for slot in range(2):
        loads.append((maps.at[slot], raw.at[MAP0 + slot, body, pl.ds(0, cols)]))
    loads.append((land, rawl.at[body, pl.ds(0, cols)]))
    loads.append((ostep, own_k))
    loads = [
        pltpu.make_async_copy(src, dst, load_sem.at[slot])
        for slot, (src, dst) in enumerate(loads)
    ]
    for copy in loads:
        copy.start()

    barrier = pltpu.get_barrier_semaphore()

    def greet(step, carry):
        pl.semaphore_signal(
            barrier, inc=1, device_id={"scen": lax.rem(me_s + step, ns)}, device_id_type=MESH
        )
        return carry

    lax.fori_loop(1, ns, greet, 0)
    for dx, dy in SIDES:

        @pl.when(there(dx, dy))
        def _(dx=dx, dy=dy):
            pl.semaphore_signal(barrier, inc=1, device_id=target(dx, dy), device_id_type=MESH)

    over_x = jnp.where(top, 0, 1) + jnp.where(bottom, 0, 1)
    over_y = jnp.where(left, 0, 1) + jnp.where(right, 0, 1)

    def row_copies(dx):
        edge = pl.ds(0, HALO) if dx < 0 else pl.ds(rows - HALO, HALO)
        halo = pl.ds(rows + SUB, HALO) if dx < 0 else pl.ds(SUB - HALO, HALO)
        across = pl.ds(0, cols)
        pairs = [
            (ref.at[0, edge, :], raw.at[slot, halo, across])
            for slot, ref in enumerate((dens, trait, var, opt, obs))
        ]
        pairs.append((maps.at[:, edge, :], raw.at[pl.ds(MAP0, 2), halo, across]))
        pairs.append((land.at[edge, :], rawl.at[halo, across]))
        pairs.append((ostep, down_k if dx < 0 else up_k))
        way = 0 if dx < 0 else 1
        return [
            pltpu.make_async_remote_copy(
                src_ref=src,
                dst_ref=dst,
                send_sem=row_send.at[way, slot],
                recv_sem=row_recv.at[way, slot],
                device_id=target(dx, 0),
                device_id_type=MESH,
            )
            for slot, (src, dst) in enumerate(pairs)
        ]

    for copy in loads:
        copy.wait()

    def field(slot, rws, cls):
        if slot == LAND:
            return rawl[rws, cls].astype(jnp.float32)
        return raw[slot, rws, cls]

    def pack(block, carry):
        rws = pl.ds(pl.multiple_of(SUB + block * SUB, SUB), SUB)
        packed = jnp.zeros((SUB, LANE), jnp.float32)
        for slot in range(8):
            pair = jnp.where(
                lane < LANE // 2,
                field(slot, rws, pl.ds(0, LANE)),
                field(slot, rws, pl.ds(cols - LANE, LANE)),
            )
            turned = pltpu.roll(pair, 8 * slot + 4, 1)
            packed = jnp.where(lane // 8 == slot, turned, packed)
        square[pl.ds(pl.multiple_of(block * SUB, SUB), SUB), :] = packed
        return carry

    lax.fori_loop(0, blocks, pack, 0, unroll=4)
    turned = jnp.transpose(square[...])
    corner = jnp.zeros((SUB, LANE), jnp.float32)
    for slot in range(8):
        part = turned[8 * slot : 8 * slot + 8, :]
        corner = jnp.where(lane // 8 == slot, pltpu.roll(part, 8 * slot + 4, 1), corner)
    for pair in range(4):
        even = turned[16 * pair : 16 * pair + 8, :]
        odd = turned[16 * pair + 8 : 16 * pair + 16, :]
        colsend[0, 8 * pair : 8 * pair + 8, :] = jnp.where(sub < 4, even, pltpu.roll(odd, 4, 0))
        colsend[1, 8 * pair : 8 * pair + 8, :] = jnp.where(sub < 4, pltpu.roll(even, 4, 0), odd)
    cornsend[...] = corner

    def prepare(block, lanes):
        src = pl.ds(pl.multiple_of(block * SUB, SUB), SUB)
        dst = pl.ds(pl.multiple_of(block * SUB + OFF - SUB, SUB), SUB)
        for tile in lanes:
            cls = pl.ds(tile * LANE, LANE)
            n, z, v = raw[DENS, src, cls], raw[TRAIT, src, cls], raw[VAR, src, cls]
            second_moment = v + z * z

            def put(name, value):
                planes[PLANE[name]][tile, dst, :] = value

            put("n0", n)
            put("q0", n * z)
            put("s0", second_moment)
            put("m0", n * second_moment)
            put("lnd", rawl[src, cls].astype(jnp.float32))
            share = 1.0 / (1.0 + jnp.exp(-raw[MAP0, src, cls]))
            rho = (0.5 * REACH_MAX) * share
            put("rho", rho)
            x = raw[MAP1, src, cls]
            small = jnp.exp(-jnp.abs(x))
            put("sel", jnp.maximum(x, 0.0) + jnp.log1p(small))
            if tile < tiles:
                put("fac0", rho * (1.0 - share))
                put("fac1", jnp.where(x >= 0.0, 1.0, small) / (1.0 + small))

    def prepare_own(block, carry):
        prepare(block, range(tiles))
        return carry


    pl.semaphore_wait(barrier, ns - 1 + (over_x + 1) * (over_y + 1) - 1)
    def col_copy(dx, dy):
        index = SIDES.index((dx, dy))
        came = SIDES.index((-dx, -dy))
        if dx == 0:
            way = 0 if dy > 0 else 1
            src, dst = colsend.at[way], colrx.at[way]
        else:
            src, dst = cornsend, cornrx.at[came]
        return pltpu.make_async_remote_copy(
            src_ref=src,
            dst_ref=dst,
            send_sem=col_send.at[index],
            recv_sem=col_recv.at[came],
            device_id=target(dx, dy),
            device_id_type=MESH,
        )

    col_sides = [side for side in SIDES if side[1]]
    for dx, dy in col_sides:

        @pl.when(there(dx, dy))
        def _(dx=dx, dy=dy):
            col_copy(dx, dy).start()

    for dx in (-1, 1):

        @pl.when(there(dx, 0))
        def _(dx=dx):
            for copy in row_copies(dx):
                copy.start()

    lax.fori_loop(1, blocks + 1, prepare_own, 0, unroll=4)

    soon = min(blocks, 2 * per_band)
    zero = jnp.zeros((SUB, LANE), jnp.float32)
    for dx, halo, kref in ((-1, 0, up_k), (1, rows + SUB, down_k)):

        @pl.when(there(dx, 0))
        def _(dx=dx):
            for copy in row_copies(-dx):
                copy.wait_recv()

        @pl.when(jnp.logical_not(there(dx, 0)))
        def _(halo=halo, kref=kref):
            for tile in range(tiles):
                cls = pl.ds(tile * LANE, LANE)
                for slot in range(7):
                    raw[slot, pl.ds(halo, SUB), cls] = zero
                rawl[pl.ds(halo, SUB), cls] = jnp.zeros((SUB, LANE), jnp.int32)
            kref[...] = jnp.zeros_like(kref)

    for dx, dy in col_sides:

        @pl.when(there(dx, dy))
        def _(dx=dx, dy=dy):
            col_copy(-dx, -dy).wait_recv()

        @pl.when(jnp.logical_not(there(dx, dy)))
        def _(dx=dx, dy=dy):
            if dx == 0:
                colrx[0 if dy < 0 else 1] = jnp.zeros((32, LANE), jnp.float32)
            else:
                cornrx[SIDES.index((dx, dy))] = zero

    for pair in range(4):
        part = pl.ds(8 * pair, 8)
        from_left, from_right = colrx[0, part, :], colrx[1, part, :]
        square[16 * pair : 16 * pair + 8, :] = jnp.where(
            sub < 4, from_left, pltpu.roll(from_right, 4, 0)
        )
        square[16 * pair + 8 : 16 * pair + 16, :] = jnp.where(
            sub < 4, pltpu.roll(from_left, 4, 0), from_right
        )
    upper = lax.rem(lane, 8) < 4
    square[64:72, :] = jnp.where(
        sub < 4,
        jnp.where(upper, cornrx[SIDES.index((-1, -1))], cornrx[SIDES.index((1, -1))]),
        jnp.where(upper, cornrx[SIDES.index((-1, 1))], cornrx[SIDES.index((1, 1))]),
    )

    def steps_of(ref):
        return jnp.broadcast_to(ref[...], (SUB, LANE)).astype(jnp.float32)

    square[72:80, :] = jnp.where(
        sub == 0,
        steps_of(own_k),
        jnp.where(sub == 1, steps_of(up_k), jnp.where(sub == 2, steps_of(down_k), 0.0)),
    )
    square[80:128, :] = jnp.zeros((48, LANE), jnp.float32)
    square[...] = jnp.transpose(square[...])

    halo_lanes = pl.ds(cols, LANE)

    def put_halo(slot, rws, value):
        if slot == LAND:
            rawl[rws, halo_lanes] = value.astype(jnp.int32)
        else:
            raw[slot, rws, halo_lanes] = value

    def unpack(block, carry):
        got = square[pl.ds(pl.multiple_of(block * SUB, SUB), SUB), :]
        rws = pl.ds(pl.multiple_of(SUB + block * SUB, SUB), SUB)
        for slot in range(8):
            put_halo(slot, rws, pltpu.roll(got, LANE - (8 * slot + 4), 1))
        krow[rws, :] = jnp.broadcast_to(got[:, 72:73], (SUB, LANE))
        return carry

    lax.fori_loop(0, soon, unpack, 0, unroll=4)
    for slot in range(8):
        got = pltpu.roll(square[8 * slot : 8 * slot + 8, :], LANE - 68, 1)
        got = pltpu.roll(got, 4, 0)
        put_halo(slot, pl.ds(0, SUB), got)
        put_halo(slot, pl.ds(rows + SUB, SUB), got)
    krow[0:SUB, :] = jnp.broadcast_to(square[rows - SUB : rows, 73:74], (SUB, LANE))
    krow[rows + SUB : rows + 2 * SUB, :] = jnp.broadcast_to(square[0:SUB, 74:75], (SUB, LANE))

    def prepare_side(block, carry):
        prepare(block, (tiles,))
        return carry

    lax.fori_loop(0, soon + 1, prepare_side, 0, unroll=3)
    prepare(0, range(tiles))

    def finish_halo():
        lax.fori_loop(soon, blocks, unpack, 0, unroll=4)
        lax.fori_loop(soon + 1, blocks + 2, prepare_side, 0, unroll=3)
        prepare(blocks + 1, range(tiles))


    def east(values):
        turned = [pltpu.roll(value, LANE - 1, 1) for value in values]
        return [
            jnp.where(lane == LANE - 1, turned[(tile + 1) % wide], turned[tile])
            for tile in range(wide)
        ]

    def west(values):
        turned = [pltpu.roll(value, 1, 1) for value in values]
        return [
            jnp.where(lane == 0, turned[(tile - 1) % wide], turned[tile])
            for tile in range(wide)
        ]

    def getter(row):
        def get(name, shift=0):
            if shift == 0:
                rws = pl.ds(pl.multiple_of(row, SUB), SUB)
            else:
                rws = pl.ds(row + shift, SUB)
            return [planes[PLANE[name]][tile, rws, :] for tile in range(wide)]

        def put(name, values):
            rws = pl.ds(pl.multiple_of(row, SUB), SUB)
            for tile, value in enumerate(values):
                planes[PLANE[name]][tile, rws, :] = value

        def get_raw(slot):
            rws = pl.ds(pl.multiple_of(row - SUB, SUB), SUB)
            return [raw[slot, rws, tile * LANE : (tile + 1) * LANE] for tile in range(wide)]

        return get, put, get_raw

    def spread(get, name, weights, keep=None, put=None):
        wx, ww, wy, wyn = weights
        here = get(name)
        ahead, behind = east(here), west(here)
        south, north = get(name, 1), get(name, -1)
        fx = [e - c for e, c in zip(ahead, here)]
        fy = [s - c for s, c in zip(south, here)]
        if keep is not None:
            put(keep, fx)
        result = [
            c + ((w * f + v * (b - c)) + (y * g + u * (n - c)))
            for c, w, f, v, b, y, g, u, n in zip(here, wx, fx, ww, behind, wy, fy, wyn, north)
        ]
        return result, fx, fy

    def pass_one(block, carry):
        row = block * SUB
        get, put, get_raw = getter(row)
        rho, lnd = get("rho"), get("lnd")
        rho_e, lnd_e = east(rho), east(lnd)
        wx = [(a + b) * (c * d) for a, b, c, d in zip(rho, rho_e, lnd, lnd_e)]
        rho_s, lnd_s = get("rho", 1), get("lnd", 1)
        wy = [(a + b) * (c * d) for a, b, c, d in zip(rho, rho_s, lnd, lnd_s)]
        rho_n, lnd_n = get("rho", -1), get("lnd", -1)
        wyn = [(a + b) * (c * d) for a, b, c, d in zip(rho, rho_n, lnd, lnd_n)]
        ww = west(wx)
        put("wx", wx)
        put("ww", ww)
        put("wy", wy)
        weights = (wx, ww, wy, wyn)
        ns_, _, _ = spread(get, "n0", weights, "fxn", put)
        qs_, _, _ = spread(get, "q0", weights, "fxq", put)
        ms_, _, _ = spread(get, "m0", weights, "fxm", put)
        z, s0, sel, optimum = get_raw(TRAIT), get("s0"), get("sel"), get_raw(OPT)
        rws = pl.ds(pl.multiple_of(row, SUB), SUB)
        for tile in range(wide):

            def one(name, value, tile=tile):
                planes[PLANE[name]][tile, rws, :] = value

            recip = 1.0 / (ns_[tile] + PRIOR)
            zs = (qs_[tile] + PRIOR * z[tile]) * recip
            ss = (ms_[tile] + PRIOR * s0[tile]) * recip
            vs = ss - zs * zs
            d = zs - optimum[tile]
            growth = lnd[tile] * (
                GROWTH - GROWTH * ns_[tile] - 0.5 * sel[tile] * (d * d + vs)
            )
            grown = jnp.exp(growth)
            n1 = ns_[tile] * grown
            response = sel[tile] * vs
            u = 1.0 / (1.0 + response)
            z1 = zs - response * u * d
            s1 = vs * u + MUTATION + z1 * z1
            one("e1", grown)
            one("r1", recip)
            one("zs1", zs)
            one("ss1", ss)
            one("u1", u)
            one("n1", n1)
            one("z1", z1)
            one("s1", s1)
            one("q1", n1 * z1)
            one("m1", n1 * s1)
        return carry

    def pass_two(block, carry):
        row = block * SUB
        get, put, get_raw = getter(row)
        weights = (get("wx"), get("ww"), get("wy"), get("wy", -1))
        ns_, _, _ = spread(get, "n1", weights, "gxn", put)
        qs_, _, _ = spread(get, "q1", weights, "gxq", put)
        ms_, _, _ = spread(get, "m1", weights, "gxm", put)
        z, s1, sel, lnd = get("z1"), get("s1"), get("sel"), get("lnd")
        optimum, observed = get_raw(OPT), get_raw(OBS)
        rws = pl.ds(pl.multiple_of(row, SUB), SUB)
        chosen = krow[pl.ds(pl.multiple_of(row - SUB, SUB), SUB), :]
        loss = jnp.where(chosen == 2.0, 2.0 * LOSS_WEIGHT, 0.0)
        for tile in range(wide):

            def one(name, value, tile=tile):
                planes[PLANE[name]][tile, rws, :] = value

            recip = 1.0 / (ns_[tile] + PRIOR)
            zs = (qs_[tile] + PRIOR * z[tile]) * recip
            ss = (ms_[tile] + PRIOR * s1[tile]) * recip
            o = optimum[tile]
            phi = ss + o * (o - 2.0 * zs)
            growth = lnd[tile] * (GROWTH - GROWTH * ns_[tile] - 0.5 * sel[tile] * phi)
            grown = jnp.exp(growth)
            n2 = ns_[tile] * grown
            a = (loss * lnd[tile]) * (n2 - observed[tile])
            g = a * n2
            gs = g * sel[tile] * recip
            lq = gs * o
            lm = -0.5 * gs
            one("lq", lq)
            one("lm", lm)
            one("ln", a * grown - 0.5 * g - (zs * lq + ss * lm))
            one("ds", -0.5 * g * phi)
        return carry

    def pass_three(block, carry):
        row = block * SUB
        get, put, get_raw = getter(row)
        weights = (get("wx"), get("ww"), get("wy"), get("wy", -1))
        spreads = []
        gx = gy = None
        for name, state, kept in (("ln", "n1", "gxn"), ("lq", "q1", "gxq"), ("lm", "m1", "gxm")):
            result, fx, fy = spread(get, name, weights)
            spreads.append(result)
            here, south = get(state), get(state, 1)
            px = [a * b for a, b in zip(fx, get(kept))]
            py = [a * (s - c) for a, s, c in zip(fy, south, here)]
            gx = px if gx is None else [a + b for a, b in zip(gx, px)]
            gy = py if gy is None else [a + b for a, b in zip(gy, py)]
        put("gx", gx)
        put("gy", gy)
        mu_n, mu_q, mu_m = spreads
        names = ("n1", "z1", "s1", "e1", "r1", "zs1", "ss1", "u1", "sel", "lnd", "lq", "lm", "ds")
        vals = {name: get(name) for name in names}
        optimum, observed = get_raw(OPT), get_raw(OBS)
        rws = pl.ds(pl.multiple_of(row, SUB), SUB)
        chosen = krow[pl.ds(pl.multiple_of(row - SUB, SUB), SUB), :]
        loss = jnp.where(chosen == 1.0, 2.0 * LOSS_WEIGHT, 0.0)
        for tile in range(wide):

            def one(name, value, tile=tile):
                planes[PLANE[name]][tile, rws, :] = value

            n1, z1, s1, grown, recip, zs, ss, u, sel, lnd, lq, lm, ds = (
                vals[name][tile] for name in names
            )
            c = mu_m[tile] * n1 + PRIOR * lm
            b = mu_q[tile] * n1 + PRIOR * lq + 2.0 * z1 * c
            a = (loss * lnd) * (n1 - observed[tile]) + (
                mu_n[tile] + mu_q[tile] * z1 + mu_m[tile] * s1
            )
            d = zs - optimum[tile]
            vs = ss - zs * zs
            g = a * n1 * lnd
            phi = d * d + vs
            dr = -(u * u) * (b * d + c * vs)
            gs = g * sel
            dd = -(gs * d + b * (1.0 - u))
            dv = c * u + dr * sel - 0.5 * gs
            kq = recip * (b + dd - 2.0 * zs * dv)
            km = recip * dv
            one("kq", kq)
            one("km", km)
            one("kn", a * grown - 0.5 * g - (zs * kq + ss * km))
            one("ds", ds + (dr * vs - 0.5 * g * phi))
        return carry

    def pass_four(block, carry):
        row = block * SUB
        get, put, _ = getter(row)
        gx, gy = get("gx"), get("gy")
        for name, state, kept in (("kn", "n0", "fxn"), ("kq", "q0", "fxq"), ("km", "m0", "fxm")):
            here = get(name)
            fx = get(kept)
            gx = [a + (e - c) * f for a, e, c, f in zip(gx, east(here), here, fx)]
            old = get(state)
            gy = [
                a + (s - c) * (t - o)
                for a, s, c, t, o in zip(gy, get(name, 1), here, get(state, 1), old)
            ]
        lnd, lnd_s = get("lnd"), get("lnd", 1)
        lnd_e = east(lnd)
        hx = [g * (a * b) for g, a, b in zip(gx, lnd, lnd_e)]
        hy = [g * (a * b) for g, a, b in zip(gy, lnd, lnd_s)]
        put("hy", hy)
        total = [a + b + c + d for a, b, c, d in zip(hx, west(hx), hy, get("hy", -1))]
        ds = get("ds")
        rws = pl.ds(pl.multiple_of(row, SUB), SUB)
        for tile in range(tiles):
            gsend[0, tile, rws, :] = -total[tile]
            gsend[1, tile, rws, :] = ds[tile]
        return carry

    def place(owner, piece):
        index = owner * pieces + piece
        return index // tiles, lax.rem(index, tiles)

    def band_rows(band, block, offset):
        return pl.ds(pl.multiple_of(offset + (band * per_band + block) * SUB, SUB), SUB)

    def scatter(band):
        def send(step, carry):
            owner = lax.rem(me_s + step, ns)
            for piece in range(pieces):
                block, tile = place(owner, piece)
                pltpu.make_async_remote_copy(
                    src_ref=gsend.at[:, tile, band_rows(band, block, OFF), :],
                    dst_ref=rrx.at[band, ns - 1 - step, piece],
                    send_sem=rs_send.at[band],
                    recv_sem=rs_recv.at[band],
                    device_id={"scen": owner},
                    device_id_type=MESH,
                ).start()
            return carry

        lax.fori_loop(1, ns, send, 0)

    def all_of(band, sem):
        return pltpu.make_async_copy(rrx.at[band], rrx.at[band], sem.at[band])

    def reduce(band):
        if ns > 1:
            all_of(band, rs_recv).wait()
        for piece in range(pieces):
            block, tile = place(me_s, piece)
            src = band_rows(band, block, OFF)
            for kind in range(2):
                terms = [gsend[kind, tile, src, :]]
                terms += [rrx[band, slot, piece, kind] for slot in range(ns - 1)]
                while len(terms) > 1:
                    pairs = [a + b for a, b in zip(terms[0::2], terms[1::2])]
                    terms = pairs + terms[len(pairs) * 2 :]
                factor = planes[PLANE["fac0"] + kind][tile, src, :]
                total[band, piece, kind] = terms[0] * factor

        def send(step, carry):
            other = lax.rem(me_s + step, ns)
            for piece in range(pieces):
                pltpu.make_async_remote_copy(
                    src_ref=total.at[band, piece],
                    dst_ref=spot(band, piece),
                    send_sem=ag_send.at[band],
                    recv_sem=ag_recv.at[band],
                    device_id={"scen": other},
                    device_id_type=MESH,
                ).start()
            return carry

        lax.fori_loop(1, ns, send, 0)
        for piece in range(pieces):
            own_copy(band, piece).start()

    def spot(band, piece):
        block, tile = place(me_s, piece)
        across = pl.ds(pl.multiple_of(tile * LANE, LANE), LANE)
        return o_grad.at[:, band_rows(band, block, 0), across]

    def own_copy(band, piece):
        return pltpu.make_async_copy(
            total.at[band, piece], spot(band, piece), own_sem.at[band, piece]
        )

    def run(step, start, stop):
        whole = (stop - start) // UNROLL

        def several(count):
            def body(index, carry):
                for part in range(count):
                    step(start + index * UNROLL + part, 0)
                return carry

            return body

        if whole > 0:
            lax.fori_loop(0, whole, several(UNROLL), 0)
        rest = (stop - start) - whole * UNROLL
        if rest > 0:
            several(rest)(jnp.int32(whole), 0)

    last = blocks + 2
    done = [1, 1, 1, 1]
    for band in range(BANDS):
        top_block = 2 + (band + 1) * per_band
        ends = [min(last + 1, top_block + lead) for lead in (3, 2, 1)] + [top_block]
        for index, step in enumerate((pass_one, pass_two, pass_three, pass_four)):
            run(step, done[index], ends[index])
        done = ends
        scatter(band)
        if band == 0:
            finish_halo()
    for band in range(BANDS):
        reduce(band)

    for dx in (-1, 1):

        @pl.when(there(dx, 0))
        def _(dx=dx):
            for copy in row_copies(dx):
                copy.wait_send()

    for dx, dy in col_sides:

        @pl.when(there(dx, dy))
        def _(dx=dx, dy=dy):
            col_copy(dx, dy).wait_send()

    for band in range(BANDS):
        if ns > 1:
            all_of(band, rs_send).wait()
            all_of(band, ag_send).wait()
            all_of(band, ag_recv).wait()
        for piece in range(pieces):
            own_copy(band, piece).wait()


def solution(mesh):
    ns, nx, ny = (mesh.shape[name] for name in ("scen", "lx", "ly"))

    def shards(density, trait, variance, optimum, observed, obs_step, land_code, maps, first, second):
        _, rows, cols = density.shape
        tiles = cols // LANE
        per_band = rows // SUB // BANDS
        pieces = per_band * tiles // ns
        f32 = jnp.float32
        shape = jax.ShapeDtypeStruct(maps.shape, f32)
        dma = pltpu.SemaphoreType.DMA
        gradient = pl.pallas_call(
            functools.partial(kernel, (ns, nx, ny, rows, cols)),
            out_shape=shape,
            in_specs=[pl.BlockSpec(memory_space=pltpu.HBM)] * 8,
            out_specs=pl.BlockSpec(memory_space=pl.ANY),
            scratch_shapes=[
                pltpu.VMEM((7, rows + 2 * SUB, cols + LANE), f32),
                pltpu.VMEM((rows + 2 * SUB, cols + LANE), jnp.int32),
                pltpu.VMEM((1, rows), jnp.int32),
                pltpu.VMEM((1, rows), jnp.int32),
                pltpu.VMEM((1, rows), jnp.int32),
                pltpu.VMEM((rows + 2 * SUB, LANE), f32),
                pltpu.VMEM((2, 32, LANE), f32),
                pltpu.VMEM((SUB, LANE), f32),
                pltpu.VMEM((2, 32, LANE), f32),
                pltpu.VMEM((8, SUB, LANE), f32),
                pltpu.VMEM((LANE, LANE), f32),
                pltpu.VMEM((2, tiles, rows + 2 * OFF, LANE), f32),
                pltpu.VMEM((BANDS, max(ns - 1, 1), pieces, 2, SUB, LANE), f32),
                pltpu.VMEM((BANDS, pieces, 2, SUB, LANE), f32),
                dma((9,)),
                dma((2, 8)),
                dma((2, 8)),
                dma((8,)),
                dma((8,)),
                dma((BANDS,)),
                dma((BANDS,)),
                dma((BANDS,)),
                dma((BANDS,)),
                dma((BANDS, pieces)),
            ]
            + [pltpu.VMEM((tiles + 1, rows + 2 * OFF, LANE), f32)] * len(NAMES),
            compiler_params=pltpu.CompilerParams(
                collective_id=0, has_side_effects=True, vmem_limit_bytes=60 * 1024 * 1024
            ),
        )(density, trait, variance, optimum, observed, obs_step, land_code, maps)
        new_first = BETA_FIRST * first + (1.0 - BETA_FIRST) * gradient
        new_second = BETA_SECOND * second + (1.0 - BETA_SECOND) * gradient * gradient
        first_hat = new_first / (1.0 - BETA_FIRST**ADAM_STEP)
        second_hat = new_second / (1.0 - BETA_SECOND**ADAM_STEP)
        new_maps = maps - LEARN_RATE * first_hat / (jnp.sqrt(second_hat) + ADAM_EPS)
        return new_maps, new_first, new_second

    tile = P("scen", "lx", "ly")
    flat = P(None, "lx", "ly")
    return jax.shard_map(
        shards,
        mesh=mesh,
        in_specs=(tile,) * 5 + (P("scen", "lx"), P("lx", "ly"), flat, flat, flat),
        out_specs=(flat, flat, flat),
        check_vma=False,
    )
```
